512 devices in a mesh: seq: 32 (over z, core), dp: 16 (over y, x).
Axes of the slice: x: 4, y: 4, z: 16, core: 2. Of those that a mesh axis runs over, the one named last changes fastest.
Arguments:
- queries: bfloat16 [16, 4096, 1024], P('dp', 'seq'), may hold values from -6 to 6
- key_vectors: bfloat16 [16, 4096, 1024], P('dp', 'seq'), may hold values from -6 to 6
- value_vectors: bfloat16 [16, 4096, 1024], P('dp', 'seq'), may hold values from -64 to 64
- log_decay: float32 [16, 4096, 16], P('dp', 'seq'), may hold values from -1 to 0, as said below
- restart: int32 [16, 4096], P('dp', 'seq'), may hold values 0 or 1
- norm_gain: float32 [1024], replicated, may hold values from 0.5 to 1.5
- upstream: bfloat16 [16, 4096, 1024], P('dp', 'seq'), may hold values from -6 to 6
Outputs:
- layer_out: bfloat16 [16, 4096, 1024], P('dp', 'seq')
- grad_query: bfloat16 [16, 4096, 1024], P('dp', 'seq')
- grad_key: bfloat16 [16, 4096, 1024], P('dp', 'seq')
- grad_value: bfloat16 [16, 4096, 1024], P('dp', 'seq')
- grad_decay: float32 [16, 4096, 16], P('dp', 'seq')
- grad_gain: float32 [1024], replicated
The draws below stay inside these ranges and needn't reach their ends.
Inputs may be any that keep to these rules, and one draw needn't show every extreme that they name: `log_decay`: never positive. `restart`: 1 marks a sample before which the state is cleared.
All inputs are finite; a program needn't handle non-finite values. No bound on the sum of `restart` on one device may be relied on, other than what follows from the above.
Results may differ from the reference program's by a relative error of at most 0.0096.
Values sent between devices are 32-bit elements; how exact they have to be, the bound alone decides.
A program may use at most 128 MiB of HBM per device.

```python
import math
import jax
import jax.numpy as jnp
from jax import lax

HEAD_TOTAL = 16
D = 1024
TOK_DEV = 128
SCAN_LENGTH = 4096
SCAN_COUNT = 16


def draw_value_vectors(key, part):
    key_base, key_rows, key_columns = jax.random.split(key, 3)
    base = jnp.clip(jax.random.normal(key_base, (SCAN_COUNT, SCAN_LENGTH, D), jnp.float32), -6.0, 6.0)
    row_scale = jnp.exp(jax.random.uniform(key_rows, (SCAN_COUNT, SCAN_LENGTH, 1), jnp.float32, -1.15, 1.15))
    column_scale = jnp.exp(jax.random.uniform(key_columns, (1, 1, D), jnp.float32, -1.15, 1.15))
    return (base * row_scale * column_scale).astype(jnp.bfloat16)


def draw_log_decay(key, part):
    key_quick, key_token, key_block, key_where, key_width = jax.random.split(key, 5)
    quick_share = 0.45
    quick = jax.random.uniform(key_quick, (SCAN_COUNT, 1, HEAD_TOTAL), jnp.float32) < quick_share
    decay_floor = jnp.where(quick, 6.0 / TOK_DEV, 0.4 / SCAN_LENGTH)
    token_decay_factor = jax.random.uniform(key_token, (SCAN_COUNT, SCAN_LENGTH, HEAD_TOTAL), jnp.float32, 0.5, 1.5)
    block_draw = jax.random.uniform(key_block, (SCAN_COUNT, SCAN_LENGTH // TOK_DEV, 1, HEAD_TOTAL), jnp.float32, 0.7, 1.4)
    block_decay_factor = jnp.repeat(block_draw, TOK_DEV, axis=2).reshape(SCAN_COUNT, SCAN_LENGTH, HEAD_TOTAL)
    places = jax.random.randint(key_where, (SCAN_COUNT, 1, 2), 0, SCAN_LENGTH)
    positions = jnp.arange(SCAN_LENGTH, dtype=jnp.int32)[None, :, None]
    reset_marks = jnp.any(positions == places, axis=2)
    reset_flags = jax.random.uniform(key_width, (SCAN_COUNT, SCAN_LENGTH, HEAD_TOTAL), jnp.float32, math.log(0.5), math.log(0.8))
    return -decay_floor * token_decay_factor * block_decay_factor + jnp.where(reset_marks[..., None], reset_flags, 0.0)


def touch_ends(drawn, own_key, low, top_value):
    dims = drawn.shape
    place = [jax.random.randint(jax.random.fold_in(own_key, axis), (), 0, dims[axis]) for axis in range(len(dims))]
    drawn = drawn.at[tuple(place)].set(low)
    longest = dims.index(max(dims))
    place[longest] = (place[longest] + 1) % dims[longest]
    return drawn.at[tuple(place)].set(top_value)


def raised(drawn, rng, source, target, blocks, factor):
    def block_of(position):
        return (jnp.arange(drawn.shape[position]) // (drawn.shape[position] // blocks)).reshape((-1,) + (1,) * (drawn.ndim - 1 - position))

    one_side = jax.random.permutation(rng, blocks)[block_of(target)]
    other_side = (block_of(target) + blocks // 2) % blocks
    return jnp.where((block_of(source) == one_side) | (block_of(source) == other_side), factor * drawn, drawn)


def block_levels(rng, dims, cuts, smallest, top_value):
    loudness, own = 1.0, jax.random.fold_in(rng, 6)
    for dim, blocks in cuts:
        heights = jnp.exp(jax.random.uniform(jax.random.fold_in(own, dim), (blocks,), jnp.float32, smallest / len(cuts), top_value / len(cuts)))
        loudness = loudness * jnp.repeat(heights, dims[dim] // blocks).reshape([-1 if axis == dim else 1 for axis in range(len(dims))])
    return loudness


def scatter_about(rng, extent, deviation, bound, cuts=(), kind=jnp.bfloat16):
    factor_of = block_levels(rng, extent, cuts, -0.22, 0.18) if cuts else 1.0
    result = jax.random.normal(rng, extent, jnp.float32) * deviation * factor_of
    return jnp.minimum(jnp.maximum(result, -bound), bound).astype(kind)


def bell_draw_with(rng, shape, scale, bound, cuts, heavy, kind=jnp.bfloat16):
    values = scale * jax.random.normal(rng, shape, jnp.float32)
    if cuts:
        values = values * block_levels(rng, shape, cuts, -0.22, 0.18)
    return jnp.clip(raised(values, jax.random.fold_in(rng, 3), *heavy), -bound, bound).astype(kind)


def setup_inputs(seed: int = 0) -> dict:
    streams_of = jax.random.split(jax.random.key(seed), 8)
    return {
        "queries": scatter_about(streams_of[0], (SCAN_COUNT, SCAN_LENGTH, D), 1.0, 6.0, ((0, 16), (1, 32))),
        "key_vectors": scatter_about(streams_of[1], (SCAN_COUNT, SCAN_LENGTH, D), 1.0, 6.0, ((0, 16), (1, 32))),
        "value_vectors": draw_value_vectors(jax.random.fold_in(streams_of[7], 71), 0),
        "log_decay": draw_log_decay(jax.random.fold_in(streams_of[7], 71), 0),
        "restart": touch_ends((jax.random.randint(streams_of[4], (SCAN_COUNT, SCAN_LENGTH), 0, 16 * TOK_DEV) < 1).astype(jnp.int32), jax.random.fold_in(streams_of[4], 1), 0, 1),
        "norm_gain": jnp.clip(1.0 + 0.1 * jax.random.normal(streams_of[5], (D,), jnp.float32), 0.5, 1.5),
        "upstream": bell_draw_with(streams_of[6], (SCAN_COUNT, SCAN_LENGTH, D), 1.0, 6.0, ((0, 16), (1, 32)), (1, 2, 32, 2.75)),
    }


EPSILON = 1e-06
EXACT = lax.Precision.HIGHEST

def blend(pattern, first_operand, second_operand):
    return jnp.einsum(pattern, first_operand.astype(jnp.float32), second_operand.astype(jnp.float32), precision=EXACT)

def exact(pattern, first_operand, second_operand):
    return jnp.einsum(pattern, first_operand, second_operand, precision=EXACT)

def split_heads(row_data, head_count):
    return row_data.reshape(row_data.shape[0], row_data.shape[1], head_count, row_data.shape[2] // head_count)

def decay_tables(log_decay, restart):
    summed = jnp.cumsum(log_decay, axis=1)
    resets = jnp.cumsum(restart, axis=1, dtype=jnp.int32)
    last_total = summed[:, -1, :]
    last_reset = resets[:, -1:]
    entry_decay = jnp.where((resets == 0)[:, :, None], jnp.exp(summed), 0.0)
    exit_decay = jnp.where((resets == last_reset)[:, :, None], jnp.exp(last_total[:, None, :] - summed), 0.0)
    block_carry = jnp.where(last_reset == 0, jnp.exp(last_total), 0.0)
    by_head = jnp.transpose(summed, (0, 2, 1))
    spread = by_head[:, :, :, None] - by_head[:, :, None, :]
    row_index = lax.broadcasted_iota(jnp.int32, spread.shape, 2)
    col_index = lax.broadcasted_iota(jnp.int32, spread.shape, 3)
    allowed = (row_index >= col_index) & (resets[:, None, :, None] == resets[:, None, None, :])
    pair_decay = jnp.exp(jnp.where(allowed, spread, -1e+30))
    return (entry_decay, exit_decay, block_carry, pair_decay)

def block_state(key_heads, value_heads, exit_decay):
    decayed_keys = key_heads.astype(jnp.float32) * exit_decay[..., None]
    return (exact('bjhe,bjhf->bhef', decayed_keys, value_heads.astype(jnp.float32)), decayed_keys)

def block_forward(query_heads, key_heads, value_heads, entry_decay, pair_decay, state_in, norm_gain, upstream_heads):
    head_count = query_heads.shape[2]
    scores = blend('bihe,bjhe->bhij', query_heads, key_heads)
    weights = (scores * pair_decay).astype(jnp.bfloat16)
    local_part = blend('bhij,bjhe->bihe', weights, value_heads)
    decayed_queries = query_heads.astype(jnp.float32) * entry_decay[..., None]
    carried_part = exact('bihe,bhef->bihf', decayed_queries, state_in)
    mixture = local_part + carried_part
    inverse = lax.rsqrt(lax.optimization_barrier(jnp.mean(mixture * mixture, axis=-1, keepdims=True)) + EPSILON)
    normed = mixture * inverse
    gain_heads = norm_gain.reshape(head_count, -1)
    layer_out = (normed * gain_heads).astype(jnp.bfloat16)
    upstream_float = upstream_heads.astype(jnp.float32)
    gain_part = lax.optimization_barrier(jnp.sum(upstream_float * normed, axis=(0, 1)))
    grad_normed = upstream_float * gain_heads
    grad_mixed = (inverse * (grad_normed - normed * lax.optimization_barrier(jnp.mean(grad_normed * normed, axis=-1, keepdims=True)))).astype(jnp.bfloat16)
    query_state = exact('bihe,bihf->bhef', decayed_queries, grad_mixed.astype(jnp.float32))
    flat_out = layer_out.reshape(layer_out.shape[0], layer_out.shape[1], -1)
    return (scores, weights, carried_part, flat_out, gain_part, grad_mixed, query_state)

def block_backward(query_heads, key_heads, value_heads, entry_decay, exit_decay, block_carry, pair_decay, scores, weights, carried_part, decayed_keys, grad_mixed, state_in, state_grad):
    grad_pairs = blend('bihe,bjhe->bhij', grad_mixed, value_heads)
    grad_weights = (grad_pairs * pair_decay).astype(jnp.bfloat16)
    mixed_float = grad_mixed.astype(jnp.float32)
    values_float = value_heads.astype(jnp.float32)
    grad_query = blend('bhij,bjhe->bihe', grad_weights, key_heads) + exact('bihf,bhef->bihe', mixed_float * entry_decay[..., None], state_in)
    grad_key = blend('bhij,bihe->bjhe', grad_weights, query_heads) + exact('bjhf,bhef->bjhe', values_float * exit_decay[..., None], state_grad)
    carried_value = exact('bjhe,bhef->bjhf', decayed_keys, state_grad)
    grad_value = blend('bhij,bihe->bjhe', weights, grad_mixed) + carried_value
    pair_terms = scores * grad_pairs * pair_decay
    balance = lax.optimization_barrier(jnp.sum(pair_terms, axis=3)) - lax.optimization_barrier(jnp.sum(pair_terms, axis=2))
    later_terms = jnp.transpose(balance, (0, 2, 1)) + lax.optimization_barrier(jnp.sum(carried_part * mixed_float, axis=-1))
    earlier_terms = lax.optimization_barrier(jnp.sum(carried_value * values_float, axis=-1))
    through = block_carry * lax.optimization_barrier(jnp.sum(state_in * state_grad, axis=(2, 3)))
    grad_decay = jnp.flip(jnp.cumsum(jnp.flip(later_terms, 1), axis=1), 1) + (jnp.cumsum(earlier_terms, axis=1) - earlier_terms) + through[:, None, :]
    row_shape = (grad_query.shape[0], grad_query.shape[1], -1)
    return (grad_query.reshape(row_shape).astype(jnp.bfloat16), grad_key.reshape(row_shape).astype(jnp.bfloat16), grad_value.reshape(row_shape).astype(jnp.bfloat16), grad_decay)

def reference(queries, key_vectors, value_vectors, log_decay, restart, norm_gain, upstream):
    block_total = SCAN_LENGTH // TOK_DEV

    def to_blocks(array):
        shaped = array.reshape((SCAN_COUNT, block_total, TOK_DEV) + array.shape[2:])
        return jnp.swapaxes(shaped, 0, 1)

    def from_blocks(array):
        return jnp.swapaxes(array, 0, 1).reshape((SCAN_COUNT, SCAN_LENGTH) + array.shape[3:])
    inputs = tuple((to_blocks(array) for array in (queries, key_vectors, value_vectors, log_decay, restart, upstream)))

    def prepare(package):
        query_rows, key_rows, value_rows, decay_rows, restart_rows, upstream_rows = package
        tables = decay_tables(decay_rows, restart_rows)
        heads_all = (split_heads(query_rows, HEAD_TOTAL), split_heads(key_rows, HEAD_TOTAL), split_heads(value_rows, HEAD_TOTAL), split_heads(upstream_rows, HEAD_TOTAL))
        return (tables, heads_all)

    def first_pass(package):
        tables, heads_all = prepare(package)
        state_part, unused_keys = block_state(heads_all[1], heads_all[2], tables[1])
        return (tables[2], state_part)
    carries, parts = lax.map(first_pass, inputs)
    zero_state = jnp.zeros(parts.shape[1:], jnp.float32)

    def forward_step(state, element):
        return (element[0][..., None, None] * state + element[1], state)
    unused_end, states_in = lax.scan(forward_step, zero_state, (carries, parts))

    def second_pass(package):
        tables, heads_all = prepare(package[:6])
        results = block_forward(heads_all[0], heads_all[1], heads_all[2], tables[0], tables[3], package[6], norm_gain, heads_all[3])
        return (results[3], results[4], results[6])
    outputs_all, gain_parts, query_states = lax.map(second_pass, inputs + (states_in,))

    def backward_step(gradient, element):
        return (element[1] + element[0][..., None, None] * gradient, gradient)
    unused_start, states_grad = lax.scan(backward_step, zero_state, (carries, query_states), reverse=True)

    def third_pass(package):
        tables, heads_all = prepare(package[:6])
        state_in = package[6]
        state_grad = package[7]
        unused_part, decayed_keys = block_state(heads_all[1], heads_all[2], tables[1])
        results = block_forward(heads_all[0], heads_all[1], heads_all[2], tables[0], tables[3], state_in, norm_gain, heads_all[3])
        return block_backward(heads_all[0], heads_all[1], heads_all[2], tables[0], tables[1], tables[2], tables[3], results[0], results[1], results[2], decayed_keys, results[5], state_in, state_grad)
    grad_query, grad_key, grad_value, grad_decay = lax.map(third_pass, inputs + (states_in, states_grad))
    grad_gain = lax.optimization_barrier(jnp.sum(gain_parts, axis=0)).reshape(-1)
    return (from_blocks(outputs_all), from_blocks(grad_query), from_blocks(grad_key), from_blocks(grad_value), from_blocks(grad_decay), grad_gain)
```

```python
import functools

import jax
import jax.numpy as jnp
from jax import lax
from jax.experimental import pallas as pl
from jax.experimental.pallas import tpu as pltpu
from jax.sharding import PartitionSpec as P

MESH = pl.DeviceIdType.MESH
HEADS = 16
PAIRS = HEADS // 2
MINE = PAIRS // 2
TOK = 128
LANES = 128
HALF = 64
CHIPS = 16
ROWS = MINE * HALF // CHIPS
EPSILON = 1e-06
F32 = jnp.float32
BF16 = jnp.bfloat16
FAR_FIRST = (8, 7, 9, 6, 10, 5, 11, 4, 12, 3, 13, 2, 14, 1, 15)


def mm(a, b):
    return jnp.dot(a, b, preferred_element_type=F32)


def mm_t(a, b):
    return lax.dot_general(a, b, (((1,), (1,)), ((), ())), preferred_element_type=F32)


def t_mm(a, b):
    return lax.dot_general(a, b, (((0,), (0,)), ((), ())), preferred_element_type=F32)


def split_mm(a, b):
    high = a.astype(BF16)
    low = (a - high.astype(F32)).astype(BF16)
    return mm(high, b) + mm(low, b)


def split_mm_left(a, b):
    high = b.astype(BF16)
    low = (b - high.astype(F32)).astype(BF16)
    return mm(a, high) + mm(a, low)


def kernel(
    q_hbm, k_hbm, v_hbm, u_hbm, ld_ref, rs_ref, gain_ref,
    out_ref, dq_ref, dk_ref, dv_ref, dd_ref, dg_ref,
    q_s, k_s, v_s, u_s, in_sem,
    entry_s, exit_s, p_s, pt_s, sp_s, spt_s, loc_s, car_s, qet_s, g_s, dkl_s, dvl_s,
    st_own, st_oth, qs_own, qs_oth, carr_own, carr_oth, si_s, si_x, sg_s, sg_x,
    send1, recv1, send2, recv2, send3, recv3, send4, recv4,
    gain_own, gain_oth, gain_z, gain_all,
    x_send, x_recv, p_send, p_recv, g_send, g_recv,
):
    seq = lax.axis_index("seq")
    dp = lax.axis_index("dp")
    z = seq // 2
    core = lax.rem(seq, 2)
    partner = z * 2 + (1 - core)

    def chip(index):
        return index * 2 + core

    barrier = pltpu.get_barrier_semaphore()
    for step in FAR_FIRST:
        pl.semaphore_signal(barrier, inc=1, device_id={"seq": chip(lax.rem(z + step, CHIPS))}, device_id_type=MESH)
    for step in range(1, 16):
        pl.semaphore_signal(barrier, inc=1, device_id={"dp": lax.rem(dp + step, 16)}, device_id_type=MESH)
    pl.semaphore_signal(barrier, inc=1, device_id={"seq": partner}, device_id_type=MESH)

    loads = [
        pltpu.make_async_copy(source, target, in_sem.at[i])
        for i, (source, target) in enumerate(((k_hbm, k_s), (v_hbm, v_s), (q_hbm, q_s), (u_hbm, u_s)))
    ]
    for load in loads:
        load.start()

    def lanes(pair):
        return slice(pair * LANES, (pair + 1) * LANES)

    row_i = lax.broadcasted_iota(jnp.int32, (TOK, TOK), 0)
    col_i = lax.broadcasted_iota(jnp.int32, (TOK, TOK), 1)
    low = col_i < HALF
    low_half = low[:HALF]
    tri = row_i >= col_i

    def both(column_a, column_b):
        return jnp.where(low, column_a, column_b)

    def stack(x):
        zero = jnp.zeros_like(x)
        return jnp.concatenate([jnp.where(low, x, zero), jnp.where(low, zero, x)], axis=0)

    def compact(x):
        return jnp.where(low_half, x[:HALF], x[HALF:])

    def block_diagonal(x):
        zero = jnp.zeros_like(x)
        return jnp.concatenate([jnp.where(low_half, x, zero), jnp.where(low_half, zero, x)], axis=0)

    marks = rs_ref[...].astype(F32)
    resets_col = jnp.sum(jnp.where(tri, marks, 0.0), axis=1, keepdims=True)
    resets_row = mm(jnp.broadcast_to(marks, (8, TOK)).astype(BF16), (row_i <= col_i).astype(BF16))[0:1]
    last_reset = resets_row[:, TOK - 1 :]
    cum = jnp.dot(tri.astype(F32), ld_ref[...], precision=lax.Precision.HIGHEST, preferred_element_type=F32)
    last_total = cum[TOK - 1 :, :]
    exit_all = jnp.where(resets_col == last_reset, jnp.exp(last_total - cum), 0.0)
    carry_all = jnp.where(last_reset == 0.0, jnp.exp(last_total), 0.0)
    for pair in range(PAIRS):
        a, b = 2 * pair, 2 * pair + 1
        exit_s[pair] = both(exit_all[:, a : a + 1], exit_all[:, b : b + 1])
        carr_own[pair : pair + 1, :] = jnp.where(low[0:1], carry_all[:, a : a + 1], carry_all[:, b : b + 1])

    loads[0].wait()
    loads[1].wait()
    for pair in range(PAIRS):
        decayed = (k_s[:, lanes(pair)].astype(F32) * exit_s[pair]).astype(BF16)
        st_own[pair] = compact(t_mm(decayed, v_s[:, lanes(pair)]))

    pl.semaphore_wait(barrier, 31)

    theirs = pl.ds(MINE * (1 - core), MINE)
    mine = pl.ds(MINE * core, MINE)

    def to_partner(source, target, index):
        return pltpu.make_async_remote_copy(
            source, target, x_send.at[index], x_recv.at[index], device_id={"seq": partner}, device_id_type=MESH
        )

    def to_chip(phase, source, target, there):
        return pltpu.make_async_remote_copy(
            source, target.at[z], p_send.at[phase, there], p_recv.at[phase, z],
            device_id={"seq": chip(there)}, device_id_type=MESH,
        )

    def from_chip(phase, source, target, there):
        return pltpu.make_async_remote_copy(
            source, target.at[there], p_send.at[phase, there], p_recv.at[phase, there],
            device_id={"seq": chip(there)}, device_id_type=MESH,
        )

    carry_swap = to_partner(carr_own, carr_oth, 0)
    state_swap = to_partner(st_own.at[theirs], st_oth, 1)
    carry_swap.start()
    state_swap.start()
    carry_swap.wait_recv()
    state_swap.wait_recv()

    first = core == 0

    def in_order(own, other):
        return jnp.where(first, own, other), jnp.where(first, other, own)

    carry_0, carry_1 = in_order(carr_own[...], carr_oth[...])
    for pair in range(MINE):
        index = MINE * core + pair
        s_0, s_1 = in_order(st_own[index], st_oth[pair])
        c_0, c_1 = in_order(carr_own[pl.ds(index, 1), :], carr_oth[pl.ds(index, 1), :])
        send1[pair * 4 : pair * 4 + 4, :ROWS, :] = (c_1 * s_0 + s_1).reshape(4, ROWS, LANES)
        send1[pair * 4 : pair * 4 + 4, ROWS:, :] = jnp.broadcast_to(c_0 * c_1, (4, 8, LANES))
    for step in FAR_FIRST:
        there = lax.rem(z + step, CHIPS)
        to_chip(0, send1.at[there], recv1, there).start()
    recv1[z] = send1[z]

    entry_all = jnp.where(resets_col == 0.0, jnp.exp(cum), 0.0)
    same = resets_col == resets_row
    allowed = tri & same
    allowed_t = (row_i <= col_i) & same
    cum_t = cum.T
    for head in range(HEADS):
        column, row = cum[:, head : head + 1], cum_t[head : head + 1, :]
        spread = column - row
        rows = slice((head % 2) * TOK, (head % 2 + 1) * TOK)
        p_s[head // 2, rows] = jnp.exp(jnp.where(allowed, spread, -1e30))
        pt_s[head // 2, rows] = jnp.exp(jnp.where(allowed_t, -spread, -1e30))
    for pair in range(PAIRS):
        a, b = 2 * pair, 2 * pair + 1
        entry_s[pair] = both(entry_all[:, a : a + 1], entry_all[:, b : b + 1])
    loads[2].wait()
    loads[3].wait()
    for pair in range(PAIRS):
        q, k, v = q_s[:, lanes(pair)], k_s[:, lanes(pair)], v_s[:, lanes(pair)]
        sp = mm_t(stack(q), k) * p_s[pair]
        sp_s[pair] = sp
        weights = sp.astype(BF16)
        v_2 = stack(v)
        loc_s[pair] = mm(weights[:TOK], v_2[:TOK]) + mm(weights[TOK:], v_2[TOK:])

    state = jnp.zeros((ROWS, LANES), F32)
    for there in range(CHIPS):

        @pl.when(z != there)
        def _():
            from_chip(0, send1.at[there], recv1, there).wait_recv()

        send2[there] = state

        @pl.when(z != there)
        def _():
            to_chip(1, send2.at[there], recv2, there).start()

        state = recv1[there, ROWS : ROWS + 1, :] * state + recv1[there, :ROWS, :]
    recv2[z] = send2[z]

    for pair in range(PAIRS):
        q, k = q_s[:, lanes(pair)], k_s[:, lanes(pair)]
        spt_s[pair] = mm_t(stack(k), q) * pt_s[pair]
        qet_s[pair] = (q.astype(F32) * entry_s[pair]).T.astype(BF16)

    for step in range(1, CHIPS):
        there = lax.rem(z + step, CHIPS)
        from_chip(1, send2.at[there], recv2, there).wait_recv()
    for pair in range(MINE):
        index = MINE * core + pair
        s_0, _ = in_order(st_own[index], st_oth[pair])
        c_0, _ = in_order(carr_own[pl.ds(index, 1), :], carr_oth[pl.ds(index, 1), :])
        arrived = recv2[pair * 4 : pair * 4 + 4].reshape(HALF, LANES)
        own, other = in_order(arrived, c_0 * arrived + s_0)
        si_s[index] = own
        si_x[pair] = other
    in_swap = to_partner(si_x, si_s.at[mine], 2)
    in_swap.start()
    in_swap.wait_recv()

    mean_of = jnp.where((row_i < HALF) == low, 1.0 / HALF, 0.0).astype(BF16)
    for pair in range(PAIRS):
        q = q_s[:, lanes(pair)]
        gain = gain_ref[:, lanes(pair)]
        carried = entry_s[pair] * mm(q, block_diagonal(si_s[pair]).astype(BF16))
        car_s[pair] = carried
        mixture = loc_s[pair] + carried
        inverse = lax.rsqrt(split_mm(mixture * mixture, mean_of) + EPSILON)
        normed = mixture * inverse
        out_ref[:, lanes(pair)] = (normed * gain).astype(BF16)
        up = u_s[:, lanes(pair)].astype(F32)
        gain_own[pair : pair + 1, :] = jnp.sum(up * normed, axis=0, keepdims=True)
        grad = up * gain
        shift = split_mm(grad * normed, mean_of)
        mixed = (inverse * (grad - normed * shift)).astype(BF16)
        g_s[pair] = mixed
        qs_own[pair] = compact(mm(qet_s[pair], mixed))

    query_swap = to_partner(qs_own.at[theirs], qs_oth, 3)
    gain_swap = to_partner(gain_own, gain_oth, 4)
    query_swap.start()
    gain_swap.start()
    query_swap.wait_recv()
    gain_swap.wait_recv()
    gain_chip = gain_own[...] + gain_oth[...]
    for pair in range(MINE):
        index = MINE * core + pair
        s_0, s_1 = in_order(qs_own[index], qs_oth[pair])
        c_0, _ = in_order(carr_own[pl.ds(index, 1), :], carr_oth[pl.ds(index, 1), :])
        send3[pair * 4 : pair * 4 + 4, :ROWS, :] = (s_0 + c_0 * s_1).reshape(4, ROWS, LANES)
        send3[pair * 4 : pair * 4 + 4, ROWS:, :] = jnp.broadcast_to(gain_chip[None], (4, 8, LANES))
    for step in FAR_FIRST:
        there = lax.rem(z + step, CHIPS)
        to_chip(2, send3.at[there], recv3, there).start()
    recv3[z] = send3[z]

    head_i = lax.broadcasted_iota(jnp.int32, (LANES, HEADS), 1)
    half_i = (lax.broadcasted_iota(jnp.int32, (LANES, HEADS), 0) >= HALF).astype(jnp.int32)
    column_i = lax.broadcasted_iota(jnp.int32, (TOK, HEADS), 1)

    def head_of(pair):
        return (head_i == 2 * pair + half_i).astype(BF16)

    later = jnp.zeros((TOK, HEADS), F32)
    for pair in range(PAIRS):
        q, k, v = q_s[:, lanes(pair)], k_s[:, lanes(pair)], v_s[:, lanes(pair)]
        mixed = g_s[pair]
        pairs = mm_t(stack(mixed), v)
        grad_weights = (pairs * p_s[pair]).astype(BF16)
        k_2 = stack(k)
        query_state = block_diagonal(si_s[pair]).astype(BF16)
        dq = mm(grad_weights[:TOK], k_2[:TOK]) + mm(grad_weights[TOK:], k_2[TOK:]) + entry_s[pair] * mm_t(mixed, query_state)
        dq_ref[:, lanes(pair)] = dq.astype(BF16)
        pairs_t = mm_t(stack(v), mixed)
        grad_weights_t = (pairs_t * pt_s[pair]).astype(BF16)
        q_2 = stack(q)
        dkl_s[pair] = mm(grad_weights_t[:TOK], q_2[:TOK]) + mm(grad_weights_t[TOK:], q_2[TOK:])
        weights_t = spt_s[pair].astype(BF16)
        g_2 = stack(mixed)
        dvl_s[pair] = mm(weights_t[:TOK], g_2[:TOK]) + mm(weights_t[TOK:], g_2[TOK:])
        balance = jnp.sum(sp_s[pair] * pairs - spt_s[pair] * pairs_t, axis=1, keepdims=True)
        later = later + jnp.where(column_i == 2 * pair, balance[:TOK], 0.0)
        later = later + jnp.where(column_i == 2 * pair + 1, balance[TOK:], 0.0)
        later = later + split_mm(car_s[pair] * mixed.astype(F32), head_of(pair))

    state = jnp.zeros((ROWS, LANES), F32)
    gain_sum = jnp.zeros((8, LANES), F32)
    for there in reversed(range(CHIPS)):

        @pl.when(z != there)
        def _():
            from_chip(2, send3.at[there], recv3, there).wait_recv()

        send4[there] = state

        @pl.when(z != there)
        def _():
            to_chip(3, send4.at[there], recv4, there).start()

        state = recv1[there, ROWS : ROWS + 1, :] * state + recv3[there, :ROWS, :]
        gain_sum = gain_sum + recv3[there, ROWS:, :]
    recv4[z] = send4[z]
    gain_z[...] = gain_sum
    gain_all[dp] = gain_sum

    def to_scan(there):
        return pltpu.make_async_remote_copy(
            gain_z, gain_all.at[dp], g_send.at[there], g_recv.at[dp], device_id={"dp": there}, device_id_type=MESH
        )

    def from_scan(there):
        return pltpu.make_async_remote_copy(
            gain_z, gain_all.at[there], g_send.at[there], g_recv.at[there], device_id={"dp": there}, device_id_type=MESH
        )

    for step in range(1, 16):
        to_scan(lax.rem(dp + step, 16)).start()

    later_sum = split_mm_left((row_i <= col_i).astype(BF16), later)

    for step in range(1, CHIPS):
        there = lax.rem(z + step, CHIPS)
        from_chip(3, send4.at[there], recv4, there).wait_recv()
    for pair in range(MINE):
        index = MINE * core + pair
        _, s_1 = in_order(qs_own[index], qs_oth[pair])
        _, c_1 = in_order(carr_own[pl.ds(index, 1), :], carr_oth[pl.ds(index, 1), :])
        arrived = recv4[pair * 4 : pair * 4 + 4].reshape(HALF, LANES)
        own, other = in_order(s_1 + c_1 * arrived, arrived)
        sg_s[index] = own
        sg_x[pair] = other
    grad_swap = to_partner(sg_x, sg_s.at[mine], 5)
    grad_swap.start()
    grad_swap.wait_recv()

    earlier = jnp.zeros((TOK + 8, HEADS), F32)
    for pair in range(PAIRS):
        k, v = k_s[:, lanes(pair)], v_s[:, lanes(pair)]
        state_grad = block_diagonal(sg_s[pair]).astype(BF16)
        dk_ref[:, lanes(pair)] = (dkl_s[pair] + exit_s[pair] * mm_t(v, state_grad)).astype(BF16)
        carried_value = exit_s[pair] * mm(k, state_grad)
        dv_ref[:, lanes(pair)] = (dvl_s[pair] + carried_value).astype(BF16)
        through = jnp.sum(si_s[pair] * sg_s[pair], axis=0, keepdims=True) * carr_own[pair : pair + 1, :]
        terms = jnp.concatenate([carried_value * v.astype(F32), jnp.broadcast_to(through, (8, LANES))], axis=0)
        earlier = earlier + split_mm(terms, head_of(pair))
    dd_ref[...] = later_sum + split_mm_left((row_i > col_i).astype(BF16), earlier[:TOK]) + earlier[TOK : TOK + 1]

    for step in range(1, 16):
        from_scan(lax.rem(dp + step, 16)).wait_recv()
    dg_ref[...] = jnp.sum(gain_all[...], axis=0)

    for swap in (carry_swap, state_swap, in_swap, query_swap, gain_swap, grad_swap):
        swap.wait_send()
    for step in range(1, CHIPS):
        there = lax.rem(z + step, CHIPS)
        for phase, (source, target) in enumerate(((send1, recv1), (send2, recv2), (send3, recv3), (send4, recv4))):
            to_chip(phase, source.at[there], target, there).wait_send()
    for step in range(1, 16):
        to_scan(lax.rem(dp + step, 16)).wait_send()


def local(queries, key_vectors, value_vectors, log_decay, restart, norm_gain, upstream):
    width = queries.shape[-1]
    vmem = pl.BlockSpec(memory_space=pltpu.VMEM)
    hbm = pl.BlockSpec(memory_space=pl.ANY)
    wide = pltpu.VMEM((TOK, width), BF16)
    table = pltpu.VMEM((PAIRS, TOK, LANES), F32)
    table_bf16 = pltpu.VMEM((PAIRS, TOK, LANES), BF16)
    double = pltpu.VMEM((PAIRS, 2 * TOK, LANES), F32)
    states = pltpu.VMEM((PAIRS, HALF, LANES), F32)
    some_states = pltpu.VMEM((MINE, HALF, LANES), F32)
    tile = pltpu.VMEM((8, LANES), F32)
    slices = pltpu.VMEM((CHIPS, ROWS, LANES), F32)
    slices_and = pltpu.VMEM((CHIPS, ROWS + 8, LANES), F32)
    dma = pltpu.SemaphoreType.DMA
    rows = jax.ShapeDtypeStruct((TOK, width), BF16)
    outs = pl.pallas_call(
        kernel,
        out_shape=(
            rows, rows, rows, rows,
            jax.ShapeDtypeStruct((TOK, HEADS), F32),
            jax.ShapeDtypeStruct((8, LANES), F32),
        ),
        in_specs=[hbm] * 4 + [vmem] * 3,
        out_specs=[vmem] * 6,
        scratch_shapes=[
            wide, wide, wide, wide, dma((4,)),
            table, table, double, double, double, double, table, table, table_bf16, table_bf16, table, table,
            states, some_states, states, some_states, tile, tile, states, some_states, states, some_states,
            slices_and, slices_and, slices, slices, slices_and, slices_and, slices, slices,
            tile, tile, tile, pltpu.VMEM((16, 8, LANES), F32),
            dma((6,)), dma((6,)), dma((4, CHIPS)), dma((4, CHIPS)), dma((16,)), dma((16,)),
        ],
        compiler_params=pltpu.CompilerParams(collective_id=0, has_side_effects=True, vmem_limit_bytes=48 * 1024 * 1024),
    )(
        queries[0], key_vectors[0], value_vectors[0], upstream[0], log_decay[0], restart, norm_gain.reshape(1, width)
    )
    layer_out, dq, dk, dv, dd, dg = outs
    return (layer_out[None], dq[None], dk[None], dv[None], dd[None], dg.reshape(-1))


def solution(mesh):
    row, narrow = P("dp", "seq", None), P("dp", "seq")
    return jax.shard_map(
        local,
        mesh=mesh,
        in_specs=(row, row, row, row, narrow, P(), row),
        out_specs=(row, row, row, row, row, P()),
        check_vma=False,
    )
```

```python
import functools

import jax
import jax.numpy as jnp
from jax import lax
from jax.experimental import pallas as pl
from jax.experimental.pallas import tpu as pltpu
from jax.sharding import PartitionSpec as P

MESH = pl.DeviceIdType.MESH
HEADS = 16
PAIRS = HEADS // 2
MINE = PAIRS // 2
TOK = 128
LANES = 128
HALF = 64
CHIPS = 16
ROWS = MINE * HALF // CHIPS
SENT = ROWS + 1
EPSILON = 1e-06
F32 = jnp.float32
BF16 = jnp.bfloat16
FAR_FIRST = (8, 7, 9, 6, 10, 5, 11, 4, 12, 3, 13, 2, 14, 1, 15)


def mm(a, b):
    return jnp.dot(a, b, preferred_element_type=F32)


def mm_t(a, b):
    return lax.dot_general(a, b, (((1,), (1,)), ((), ())), preferred_element_type=F32)


def t_mm(a, b):
    return lax.dot_general(a, b, (((0,), (0,)), ((), ())), preferred_element_type=F32)


def split_mm(a, b):
    high = a.astype(BF16)
    low = (a - high.astype(F32)).astype(BF16)
    return mm(high, b) + mm(low, b)


def split_mm_left(a, b):
    high = b.astype(BF16)
    low = (b - high.astype(F32)).astype(BF16)
    return mm(a, high) + mm(a, low)


def row_peer(dp, step):
    return dp // 4 * 4 + lax.rem(dp + step, 4)


def column_peer(dp, step):
    return lax.rem(dp + 4 * step, 16)


def kernel(
    q_hbm, k_hbm, v_hbm, u_hbm, ld_hbm, rs_hbm, gain_hbm,
    out_ref, dq_ref, dk_ref, dv_ref, dd_ref, dg_ref,
    q_s, k_s, v_s, u_s, ld_ref, rs_ref, gain_ref, in_sem,
    entry_s, exit_s, p_s, pt_s, sp_s, spt_s, loc_s, car_s, qet_s, g_s, dkl_s, dvl_s,
    st_own, st_oth, qs_own, qs_oth, carr_own, carr_oth, si_s, si_x, sg_s, sg_x,
    send1, recv1, send2, recv2, send3, recv3, send4, recv4,
    gain_own, gain_oth, gain_out, gain_in,
    x_send, x_recv, p_send, p_recv, g_send, g_recv,
):
    seq = lax.axis_index("seq")
    dp = lax.axis_index("dp")
    z = seq // 2
    core = lax.rem(seq, 2)
    partner = z * 2 + (1 - core)

    def chip(index):
        return index * 2 + core

    barrier = pltpu.get_barrier_semaphore()
    for step in FAR_FIRST:
        pl.semaphore_signal(barrier, inc=1, device_id={"seq": chip(lax.rem(z + step, CHIPS))}, device_id_type=MESH)
    for step in range(1, 4):
        for there in (row_peer(dp, step), column_peer(dp, step)):
            pl.semaphore_signal(barrier, inc=1, device_id={"dp": there}, device_id_type=MESH)
    pl.semaphore_signal(barrier, inc=1, device_id={"seq": partner}, device_id_type=MESH)

    loads = [
        pltpu.make_async_copy(source, target, in_sem.at[i])
        for i, (source, target) in enumerate(
            ((ld_hbm, ld_ref), (rs_hbm, rs_ref), (k_hbm, k_s), (v_hbm, v_s), (q_hbm, q_s), (u_hbm, u_s), (gain_hbm, gain_ref))
        )
    ]
    for load in loads:
        load.start()

    def lanes(pair):
        if isinstance(pair, int):
            return slice(pair * LANES, (pair + 1) * LANES)
        return pl.ds(pl.multiple_of(pair * LANES, LANES), LANES)

    row_i = lax.broadcasted_iota(jnp.int32, (TOK, TOK), 0)
    col_i = lax.broadcasted_iota(jnp.int32, (TOK, TOK), 1)
    low = col_i < HALF
    low_half = low[:HALF]
    tri = row_i >= col_i

    def both(column_a, column_b):
        return jnp.where(low, column_a, column_b)

    def stack(x):
        zero = jnp.zeros_like(x)
        return jnp.concatenate([jnp.where(low, x, zero), jnp.where(low, zero, x)], axis=0)

    def compact(x):
        return jnp.where(low_half, x[:HALF], x[HALF:])

    def block_diagonal(x):
        zero = jnp.zeros_like(x)
        return jnp.concatenate([jnp.where(low_half, x, zero), jnp.where(low_half, zero, x)], axis=0)

    loads[0].wait()
    loads[1].wait()
    marks = rs_ref[...].astype(F32)
    resets_col = jnp.sum(jnp.where(tri, marks, 0.0), axis=1, keepdims=True)
    resets_row = mm(jnp.broadcast_to(marks, (8, TOK)).astype(BF16), (row_i <= col_i).astype(BF16))[0:1]
    last_reset = resets_row[:, TOK - 1 :]
    cum_t = jnp.dot(
        ld_ref[...], (row_i <= col_i).astype(F32), precision=lax.Precision.HIGHEST, preferred_element_type=F32
    )
    cum = cum_t.T
    last_total = cum[TOK - 1 :, :]
    exit_all = jnp.where(resets_col == last_reset, jnp.exp(last_total - cum), 0.0)
    carry_all = jnp.where(last_reset == 0.0, jnp.exp(last_total), 0.0)
    for pair in range(PAIRS):
        a, b = 2 * pair, 2 * pair + 1
        exit_s[pair] = both(exit_all[:, a : a + 1], exit_all[:, b : b + 1])
        carr_own[pair : pair + 1, :] = jnp.where(low[0:1], carry_all[:, a : a + 1], carry_all[:, b : b + 1])

    loads[2].wait()
    loads[3].wait()
    for pair in range(PAIRS):
        decayed = (k_s[:, lanes(pair)].astype(F32) * exit_s[pair]).astype(BF16)
        st_own[pair] = compact(t_mm(decayed, v_s[:, lanes(pair)]))

    pl.semaphore_wait(barrier, 22)

    group = z // 4
    far_pairs = [lax.rem(group + step, 4) for step in (2, 1, 3, 0)]
    near_pairs = far_pairs[::-1]

    def to_partner(source, target, index):
        return pltpu.make_async_remote_copy(
            source, target, x_send.at[index], x_recv.at[index], device_id={"seq": partner}, device_id_type=MESH
        )

    def to_chip(phase, source, target, there):
        return pltpu.make_async_remote_copy(
            source, target.at[z], p_send.at[phase, there], p_recv.at[phase, z],
            device_id={"seq": chip(there)}, device_id_type=MESH,
        )

    def from_chip(phase, source, target, there):
        return pltpu.make_async_remote_copy(
            source, target.at[there], p_send.at[phase, there], p_recv.at[phase, there],
            device_id={"seq": chip(there)}, device_id_type=MESH,
        )

    first = core == 0

    def in_order(own, other):
        return jnp.where(first, own, other), jnp.where(first, other, own)

    carry_swap = to_partner(carr_own, carr_oth, 0)
    state_swaps = [to_partner(st_own.at[MINE * (1 - core) + pair], st_oth.at[pair], 1 + i) for i, pair in enumerate(far_pairs)]
    carry_swap.start()
    for swap in state_swaps:
        swap.start()
    carry_swap.wait_recv()

    def carries(pair):
        index = pl.ds(MINE * core + pair, 1)
        return in_order(carr_own[index, :], carr_oth[index, :])

    def start_slices(phase, pair, source, target):
        for i in range(4):
            there = pair * 4 + i

            @pl.when(there != z)
            def _():
                to_chip(phase, source.at[there], target, there).start()

    for pair, swap in zip(far_pairs, state_swaps):
        swap.wait_recv()
        s_0, s_1 = in_order(st_own[MINE * core + pair], st_oth[pair])
        c_0, c_1 = carries(pair)
        send1[pl.ds(pair * 4, 4), :ROWS, :] = (c_1 * s_0 + s_1).reshape(4, ROWS, LANES)
        send1[pl.ds(pair * 4, 4), ROWS:, :] = jnp.broadcast_to(c_0 * c_1, (4, 8, LANES))
        start_slices(0, pair, send1.at[:, pl.ds(0, SENT)], recv1.at[:, pl.ds(0, SENT)])
    recv1[z] = send1[z]

    entry_all = jnp.where(resets_col == 0.0, jnp.exp(cum), 0.0)
    same = resets_col == resets_row
    allowed = tri & same
    allowed_t = (row_i <= col_i) & same
    for head in range(HEADS):
        column, row = cum[:, head : head + 1], cum_t[head : head + 1, :]
        spread = column - row
        rows = slice((head % 2) * TOK, (head % 2 + 1) * TOK)
        p_s[head // 2, rows] = jnp.exp(jnp.where(allowed, spread, -1e30))
        pt_s[head // 2, rows] = jnp.exp(jnp.where(allowed_t, -spread, -1e30))
    for pair in range(PAIRS):
        a, b = 2 * pair, 2 * pair + 1
        entry_s[pair] = both(entry_all[:, a : a + 1], entry_all[:, b : b + 1])
    loads[4].wait()
    loads[5].wait()
    loads[6].wait()
    for pair in range(PAIRS):
        q, k, v = q_s[:, lanes(pair)], k_s[:, lanes(pair)], v_s[:, lanes(pair)]
        sp = mm_t(stack(q), k) * p_s[pair]
        sp_s[pair] = sp
        weights = sp.astype(BF16)
        v_2 = stack(v)
        loc_s[pair] = mm(weights[:TOK], v_2[:TOK]) + mm(weights[TOK:], v_2[TOK:])

    state = jnp.zeros((ROWS, LANES), F32)
    for there in range(CHIPS):

        @pl.when(z != there)
        def _():
            from_chip(0, send1.at[there, pl.ds(0, SENT)], recv1.at[:, pl.ds(0, SENT)], there).wait_recv()

        send2[there] = state

        @pl.when(z != there)
        def _():
            to_chip(1, send2.at[there], recv2, there).start()

        state = recv1[there, ROWS : ROWS + 1, :] * state + recv1[there, :ROWS, :]
    recv2[z] = send2[z]

    for pair in range(PAIRS):
        q, k = q_s[:, lanes(pair)], k_s[:, lanes(pair)]
        spt_s[pair] = mm_t(stack(k), q) * pt_s[pair]
        qet_s[pair] = (q.astype(F32) * entry_s[pair]).T.astype(BF16)

    def wait_slices(phase, pair, source, target):
        for i in range(4):
            there = pair * 4 + i

            @pl.when(there != z)
            def _():
                from_chip(phase, source.at[there], target, there).wait_recv()

    in_swaps = []
    for i, pair in enumerate(near_pairs):
        wait_slices(1, pair, send2, recv2)
        index = MINE * core + pair
        s_0, _ = in_order(st_own[index], st_oth[pair])
        c_0, _ = carries(pair)
        arrived = recv2[pl.ds(pair * 4, 4)].reshape(HALF, LANES)
        own, other = in_order(arrived, c_0 * arrived + s_0)
        si_s[index] = own
        si_x[pair] = other
        in_swaps.append(to_partner(si_x.at[pair], si_s.at[index], 5 + i))
        in_swaps[-1].start()

    mean_of = jnp.where((row_i < HALF) == low, 1.0 / HALF, 0.0).astype(BF16)
    def mix(pair):
        q = q_s[:, lanes(pair)]
        gain = gain_ref[pl.ds(pair, 1), :]
        carried = entry_s[pair] * mm(q, block_diagonal(si_s[pair]).astype(BF16))
        car_s[pair] = carried
        mixture = loc_s[pair] + carried
        inverse = lax.rsqrt(split_mm(mixture * mixture, mean_of) + EPSILON)
        normed = mixture * inverse
        out_ref[:, lanes(pair)] = (normed * gain).astype(BF16)
        up = u_s[:, lanes(pair)].astype(F32)
        gain_own[pl.ds(pair, 1), :] = jnp.sum(up * normed, axis=0, keepdims=True)
        grad = up * gain
        shift = split_mm(grad * normed, mean_of)
        mixed = (inverse * (grad - normed * shift)).astype(BF16)
        g_s[pair] = mixed
        qs_own[pair] = compact(mm(qet_s[pair], mixed))

    for pair in range(MINE):
        mix(MINE * core + pair)
    for swap in in_swaps:
        swap.wait_recv()
    for pair in range(MINE):
        mix(MINE * (1 - core) + pair)

    query_swaps = [to_partner(qs_own.at[MINE * (1 - core) + pair], qs_oth.at[pair], 9 + i) for i, pair in enumerate(far_pairs)]
    gain_swap = to_partner(gain_own, gain_oth, 13)
    for swap in query_swaps:
        swap.start()
    gain_swap.start()
    for pair, swap in zip(far_pairs, query_swaps):
        swap.wait_recv()
        s_0, s_1 = in_order(qs_own[MINE * core + pair], qs_oth[pair])
        c_0, _ = carries(pair)
        send3[pl.ds(pair * 4, 4)] = (s_0 + c_0 * s_1).reshape(4, ROWS, LANES)
        start_slices(2, pair, send3, recv3)
    recv3[z] = send3[z]

    places = (lax.rem(dp, 4), dp // 4, lax.rem(z, 4), group)

    def gain_copies(level, arriving):
        copies = []
        for step in range(1, 4):
            if level == 0:
                target = {"dp": row_peer(dp, step)}
            elif level == 1:
                target = {"dp": column_peer(dp, step)}
            elif level == 2:
                target = {"seq": chip(group * 4 + lax.rem(z + step, 4))}
            else:
                target = {"seq": chip(lax.rem(z + 4 * step, CHIPS))}
            there = lax.rem(places[level] + step, 4)
            slot = there if arriving else places[level]
            copies.append(
                pltpu.make_async_remote_copy(
                    gain_out.at[level], gain_in.at[level, slot], g_send.at[level, there], g_recv.at[level, slot],
                    device_id=target, device_id_type=MESH,
                )
            )
        return copies

    def send_gain(level, value):
        gain_out[level] = value
        gain_in[level, places[level]] = value
        for copy in gain_copies(level, False):
            copy.start()

    def gain_arrived(level):
        for copy in gain_copies(level, True):
            copy.wait_recv()
        return jnp.sum(gain_in[level], axis=0)

    gain_swap.wait_recv()
    send_gain(0, gain_own[...] + gain_oth[...])

    head_i = lax.broadcasted_iota(jnp.int32, (LANES, HEADS), 1)
    half_i = (lax.broadcasted_iota(jnp.int32, (LANES, HEADS), 0) >= HALF).astype(jnp.int32)
    column_i = lax.broadcasted_iota(jnp.int32, (TOK, HEADS), 1)

    def head_of(pair):
        return (head_i == 2 * pair + half_i).astype(BF16)

    later = jnp.zeros((TOK, HEADS), F32)
    for pair in range(PAIRS):
        if pair == MINE:
            send_gain(1, gain_arrived(0))
        q, k, v = q_s[:, lanes(pair)], k_s[:, lanes(pair)], v_s[:, lanes(pair)]
        mixed = g_s[pair]
        pairs = mm_t(stack(mixed), v)
        grad_weights = (pairs * p_s[pair]).astype(BF16)
        k_2 = stack(k)
        query_state = block_diagonal(si_s[pair]).astype(BF16)
        dq = mm(grad_weights[:TOK], k_2[:TOK]) + mm(grad_weights[TOK:], k_2[TOK:]) + entry_s[pair] * mm_t(mixed, query_state)
        dq_ref[:, lanes(pair)] = dq.astype(BF16)
        pairs_t = mm_t(stack(v), mixed)
        grad_weights_t = (pairs_t * pt_s[pair]).astype(BF16)
        q_2 = stack(q)
        dkl_s[pair] = mm(grad_weights_t[:TOK], q_2[:TOK]) + mm(grad_weights_t[TOK:], q_2[TOK:])
        weights_t = spt_s[pair].astype(BF16)
        g_2 = stack(mixed)
        dvl_s[pair] = mm(weights_t[:TOK], g_2[:TOK]) + mm(weights_t[TOK:], g_2[TOK:])
        balance = jnp.sum(sp_s[pair] * pairs - spt_s[pair] * pairs_t, axis=1, keepdims=True)
        later = later + jnp.where(column_i == 2 * pair, balance[:TOK], 0.0)
        later = later + jnp.where(column_i == 2 * pair + 1, balance[TOK:], 0.0)
        later = later + split_mm(car_s[pair] * mixed.astype(F32), head_of(pair))

    send_gain(2, gain_arrived(1))

    state = jnp.zeros((ROWS, LANES), F32)
    for there in reversed(range(CHIPS)):

        @pl.when(z != there)
        def _():
            from_chip(2, send3.at[there], recv3, there).wait_recv()

        send4[there] = state
        state = recv1[there, ROWS : ROWS + 1, :] * state + recv3[there]
    for there in range(CHIPS):

        @pl.when(z != there)
        def _():
            to_chip(3, send4.at[there], recv4, there).start()

    recv4[z] = send4[z]
    send_gain(3, gain_arrived(2))

    later_sum = split_mm_left((row_i <= col_i).astype(BF16), later)

    grad_swaps = []
    for i, pair in enumerate(near_pairs):
        wait_slices(3, pair, send4, recv4)
        index = MINE * core + pair
        _, s_1 = in_order(qs_own[index], qs_oth[pair])
        _, c_1 = carries(pair)
        arrived = recv4[pl.ds(pair * 4, 4)].reshape(HALF, LANES)
        own, other = in_order(s_1 + c_1 * arrived, arrived)
        sg_s[index] = own
        sg_x[pair] = other
        grad_swaps.append(to_partner(sg_x.at[pair], sg_s.at[index], 14 + i))
        grad_swaps[-1].start()

    earlier = jnp.zeros((TOK + 8, HEADS), F32)

    def finish(pair, earlier):
        k, v = k_s[:, lanes(pair)], v_s[:, lanes(pair)]
        state_grad = block_diagonal(sg_s[pair]).astype(BF16)
        dk_ref[:, lanes(pair)] = (dkl_s[pair] + exit_s[pair] * mm_t(v, state_grad)).astype(BF16)
        carried_value = exit_s[pair] * mm(k, state_grad)
        dv_ref[:, lanes(pair)] = (dvl_s[pair] + carried_value).astype(BF16)
        through = jnp.sum(si_s[pair] * sg_s[pair], axis=0, keepdims=True) * carr_own[pl.ds(pair, 1), :]
        terms = jnp.concatenate([carried_value * v.astype(F32), jnp.broadcast_to(through, (8, LANES))], axis=0)
        return earlier + split_mm(terms, head_of(pair))

    for pair in range(MINE):
        earlier = finish(MINE * core + pair, earlier)
    for swap in grad_swaps:
        swap.wait_recv()
    for pair in range(MINE):
        earlier = finish(MINE * (1 - core) + pair, earlier)
    total = later_sum + split_mm_left((row_i > col_i).astype(BF16), earlier[:TOK]) + earlier[TOK : TOK + 1]
    dd_ref[...] = total.T
    dg_ref[...] = gain_arrived(3)

    for swap in (carry_swap, gain_swap, *state_swaps, *in_swaps, *query_swaps, *grad_swaps):
        swap.wait_send()
    for step in range(1, CHIPS):
        there = lax.rem(z + step, CHIPS)
        to_chip(0, send1.at[there, pl.ds(0, SENT)], recv1.at[:, pl.ds(0, SENT)], there).wait_send()
        for phase, source, target in ((1, send2, recv2), (2, send3, recv3), (3, send4, recv4)):
            to_chip(phase, source.at[there], target, there).wait_send()
    for level in range(4):
        for copy in gain_copies(level, False):
            copy.wait_send()


def write_out(*refs):
    sources, targets, sem = refs[:6], refs[6:12], refs[12]
    copies = [pltpu.make_async_copy(source, target, sem.at[i]) for i, (source, target) in enumerate(zip(sources, targets))]
    for copy in copies:
        copy.start()
    for copy in copies:
        copy.wait()


def local(queries, key_vectors, value_vectors, log_decay, restart, norm_gain, upstream):
    width = queries.shape[-1]
    vmem = pl.BlockSpec(memory_space=pltpu.VMEM)
    hbm = pl.BlockSpec(memory_space=pltpu.HBM)
    wide = pltpu.VMEM((TOK, width), BF16)
    table = pltpu.VMEM((PAIRS, TOK, LANES), F32)
    table_bf16 = pltpu.VMEM((PAIRS, TOK, LANES), BF16)
    double = pltpu.VMEM((PAIRS, 2 * TOK, LANES), F32)
    states = pltpu.VMEM((PAIRS, HALF, LANES), F32)
    some_states = pltpu.VMEM((MINE, HALF, LANES), F32)
    tile = pltpu.VMEM((8, LANES), F32)
    slices = pltpu.VMEM((CHIPS, ROWS, LANES), F32)
    slices_and = pltpu.VMEM((CHIPS, ROWS + 8, LANES), F32)
    dma = pltpu.SemaphoreType.DMA
    rows = jax.ShapeDtypeStruct((TOK, width), BF16)
    results = (
        rows, rows, rows, rows,
        jax.ShapeDtypeStruct((HEADS, TOK), F32),
        jax.ShapeDtypeStruct((8, LANES), F32),
    )
    outs = pl.pallas_call(
        kernel,
        out_shape=results,
        in_specs=[hbm] * 7,
        out_specs=[vmem] * 6,
        scratch_shapes=[
            wide, wide, wide, wide,
            pltpu.VMEM((HEADS, TOK), F32), pltpu.VMEM((1, TOK), jnp.int32), tile, dma((7,)),
            table, table, double, double, double, double, table, table, table_bf16, table_bf16, table, table,
            states, some_states, states, some_states, tile, tile, states, some_states, states, some_states,
            slices_and, slices_and, slices, slices, slices, slices, slices, slices,
            tile, tile, pltpu.VMEM((4, 8, LANES), F32), pltpu.VMEM((4, 4, 8, LANES), F32),
            dma((18,)), dma((18,)), dma((4, CHIPS)), dma((4, CHIPS)), dma((4, 4)), dma((4, 4)),
        ],
        compiler_params=pltpu.CompilerParams(collective_id=0, has_side_effects=True, vmem_limit_bytes=32 * 1024 * 1024),
    )(
        *(
            pltpu.with_memory_space_constraint(array, pltpu.HBM)
            for array in (
                queries[0], key_vectors[0], value_vectors[0], upstream[0],
                log_decay[0].T, restart, norm_gain.reshape(8, LANES),
            )
        )
    )
    layer_out, dq, dk, dv, dd, dg = pl.pallas_call(
        write_out,
        out_shape=tuple(pltpu.HBM(result.shape, result.dtype) for result in results),
        in_specs=[vmem] * 6,
        out_specs=[hbm] * 6,
        scratch_shapes=[dma((6,))],
    )(*(pltpu.with_memory_space_constraint(array, pltpu.VMEM) for array in outs))
    return (layer_out[None], dq[None], dk[None], dv[None], dd.T[None], dg.reshape(-1))


def solution(mesh):
    row, narrow = P("dp", "seq", None), P("dp", "seq")
    return jax.shard_map(
        local,
        mesh=mesh,
        in_specs=(row, row, row, row, narrow, P(), row),
        out_specs=(row, row, row, row, row, P()),
        check_vma=False,
    )
```

```python
import functools

import jax
import jax.numpy as jnp
from jax import lax
from jax.experimental import pallas as pl
from jax.experimental.pallas import tpu as pltpu
from jax.sharding import PartitionSpec as P

MESH = pl.DeviceIdType.MESH
HEADS = 16
PAIRS = HEADS // 2
MINE = PAIRS // 2
TOK = 128
LANES = 128
HALF = 64
CHIPS = 16
ROWS = MINE * HALF // CHIPS
SENT = ROWS + 1
EPSILON = 1e-06
F32 = jnp.float32
BF16 = jnp.bfloat16
FAR_FIRST = (8, 7, 9, 6, 10, 5, 11, 4, 12, 3, 13, 2, 14, 1, 15)


def mm(a, b):
    return jnp.dot(a, b, preferred_element_type=F32)


def mm_t(a, b):
    return lax.dot_general(a, b, (((1,), (1,)), ((), ())), preferred_element_type=F32)


def t_mm(a, b):
    return lax.dot_general(a, b, (((0,), (0,)), ((), ())), preferred_element_type=F32)


def split_mm(a, b):
    high = a.astype(BF16)
    low = (a - high.astype(F32)).astype(BF16)
    return mm(high, b) + mm(low, b)


def split_mm_left(a, b):
    high = b.astype(BF16)
    low = (b - high.astype(F32)).astype(BF16)
    return mm(a, high) + mm(a, low)


def row_peer(dp, step):
    return dp // 4 * 4 + lax.rem(dp + step, 4)


def column_peer(dp, step):
    return lax.rem(dp + 4 * step, 16)


def kernel(
    q_hbm, k_hbm, v_hbm, u_hbm, ld_hbm, rs_hbm, gain_hbm,
    out_ref, dq_ref, dk_ref, dv_ref, dd_ref, dg_ref,
    q_s, k_s, v_s, u_s, ld_ref, rs_ref, gain_ref, in_sem,
    entry_s, exit_s, p_s, pt_s, sp_s, spt_s, loc_s, car_s, qet_s, g_s, dkl_s, dvl_s,
    st_own, st_oth, qs_own, qs_oth, carr_own, carr_oth, si_s, si_x, sg_s, sg_x,
    send1, recv1, send2, recv2, send3, recv3, send4, recv4,
    gain_own, gain_oth, gain_out, gain_in,
    x_send, x_recv, p_send, p_recv, g_send, g_recv,
):
    seq = lax.axis_index("seq")
    dp = lax.axis_index("dp")
    z = seq // 2
    core = lax.rem(seq, 2)
    partner = z * 2 + (1 - core)

    def chip(index):
        return index * 2 + core

    loads = [
        pltpu.make_async_copy(source, target, in_sem.at[i])
        for i, (source, target) in enumerate(
            ((ld_hbm, ld_ref), (rs_hbm, rs_ref), (k_hbm, k_s), (v_hbm, v_s), (q_hbm, q_s), (u_hbm, u_s), (gain_hbm, gain_ref))
        )
    ]
    for load in loads:
        load.start()

    barrier = pltpu.get_barrier_semaphore()
    for step in FAR_FIRST:
        pl.semaphore_signal(barrier, inc=1, device_id={"seq": chip(lax.rem(z + step, CHIPS))}, device_id_type=MESH)
    for step in range(1, 4):
        for there in (row_peer(dp, step), column_peer(dp, step)):
            pl.semaphore_signal(barrier, inc=1, device_id={"dp": there}, device_id_type=MESH)
    pl.semaphore_signal(barrier, inc=1, device_id={"seq": partner}, device_id_type=MESH)

    def lanes(pair):
        if isinstance(pair, int):
            return slice(pair * LANES, (pair + 1) * LANES)
        return pl.ds(pl.multiple_of(pair * LANES, LANES), LANES)

    row_i = lax.broadcasted_iota(jnp.int32, (TOK, TOK), 0)
    col_i = lax.broadcasted_iota(jnp.int32, (TOK, TOK), 1)
    low = col_i < HALF
    low_half = low[:HALF]
    tri = row_i >= col_i

    def both(column_a, column_b):
        return jnp.where(low, column_a, column_b)

    def stack(x):
        zero = jnp.zeros_like(x)
        return jnp.concatenate([jnp.where(low, x, zero), jnp.where(low, zero, x)], axis=0)

    def compact(x):
        return jnp.where(low_half, x[:HALF], x[HALF:])

    def block_diagonal(x):
        zero = jnp.zeros_like(x)
        return jnp.concatenate([jnp.where(low_half, x, zero), jnp.where(low_half, zero, x)], axis=0)

    loads[0].wait()
    loads[1].wait()
    marks = rs_ref[...].astype(F32)
    resets_col = jnp.sum(jnp.where(tri, marks, 0.0), axis=1, keepdims=True)
    resets_row = mm(jnp.broadcast_to(marks, (8, TOK)).astype(BF16), (row_i <= col_i).astype(BF16))[0:1]
    last_reset = resets_row[:, TOK - 1 :]
    cum_t = jnp.dot(
        ld_ref[...], (row_i <= col_i).astype(F32), precision=lax.Precision.HIGHEST, preferred_element_type=F32
    )
    cum = cum_t.T
    last_total = cum[TOK - 1 :, :]
    exit_all = jnp.where(resets_col == last_reset, jnp.exp(last_total - cum), 0.0)
    carry_all = jnp.where(last_reset == 0.0, jnp.exp(last_total), 0.0)
    for pair in range(PAIRS):
        a, b = 2 * pair, 2 * pair + 1
        exit_s[pair] = both(exit_all[:, a : a + 1], exit_all[:, b : b + 1])
        carr_own[pair : pair + 1, :] = jnp.where(low[0:1], carry_all[:, a : a + 1], carry_all[:, b : b + 1])

    loads[2].wait()
    loads[3].wait()
    for pair in range(PAIRS):
        decayed = (k_s[:, lanes(pair)].astype(F32) * exit_s[pair]).astype(BF16)
        st_own[pair] = compact(t_mm(decayed, v_s[:, lanes(pair)]))

    pl.semaphore_wait(barrier, 22)

    group = z // 4
    far_pairs = [lax.rem(group + step, 4) for step in (2, 1, 3, 0)]
    near_pairs = far_pairs[::-1]

    def to_partner(source, target, index):
        return pltpu.make_async_remote_copy(
            source, target, x_send.at[index], x_recv.at[index], device_id={"seq": partner}, device_id_type=MESH
        )

    def to_chip(phase, source, target, there):
        return pltpu.make_async_remote_copy(
            source, target.at[z], p_send.at[phase, there], p_recv.at[phase, z],
            device_id={"seq": chip(there)}, device_id_type=MESH,
        )

    def from_chip(phase, source, target, there):
        return pltpu.make_async_remote_copy(
            source, target.at[there], p_send.at[phase, there], p_recv.at[phase, there],
            device_id={"seq": chip(there)}, device_id_type=MESH,
        )

    first = core == 0

    def in_order(own, other):
        return jnp.where(first, own, other), jnp.where(first, other, own)

    carry_swap = to_partner(carr_own, carr_oth, 0)
    state_swaps = [to_partner(st_own.at[MINE * (1 - core) + pair], st_oth.at[pair], 1 + i) for i, pair in enumerate(far_pairs)]
    carry_swap.start()
    for swap in state_swaps:
        swap.start()
    carry_swap.wait_recv()

    def carries(pair):
        index = pl.ds(MINE * core + pair, 1)
        return in_order(carr_own[index, :], carr_oth[index, :])

    unsent = (CHIPS - 1, 0, 0, CHIPS - 1)

    def start_slices(phase, pair, source, target):
        for i in range(4):
            there = pair * 4 + i

            @pl.when((there != z) & (z != unsent[phase]))
            def _():
                to_chip(phase, source.at[there], target, there).start()

    for pair, swap in zip(far_pairs, state_swaps):
        swap.wait_recv()
        s_0, s_1 = in_order(st_own[MINE * core + pair], st_oth[pair])
        c_0, c_1 = carries(pair)
        send1[pl.ds(pair * 4, 4), :ROWS, :] = (c_1 * s_0 + s_1).reshape(4, ROWS, LANES)
        send1[pl.ds(pair * 4, 4), ROWS:, :] = jnp.broadcast_to(c_0 * c_1, (4, 8, LANES))
        start_slices(0, pair, send1.at[:, pl.ds(0, SENT)], recv1.at[:, pl.ds(0, SENT)])
    recv1[z] = send1[z]

    entry_all = jnp.where(resets_col == 0.0, jnp.exp(cum), 0.0)
    same = resets_col == resets_row
    allowed = tri & same
    allowed_t = (row_i <= col_i) & same
    for head in range(HEADS):
        column, row = cum[:, head : head + 1], cum_t[head : head + 1, :]
        spread = column - row
        rows = slice((head % 2) * TOK, (head % 2 + 1) * TOK)
        p_s[head // 2, rows] = jnp.exp(jnp.where(allowed, spread, -1e30))
        pt_s[head // 2, rows] = jnp.exp(jnp.where(allowed_t, -spread, -1e30))
    for pair in range(PAIRS):
        a, b = 2 * pair, 2 * pair + 1
        entry_s[pair] = both(entry_all[:, a : a + 1], entry_all[:, b : b + 1])
    loads[4].wait()
    loads[5].wait()
    loads[6].wait()
    for pair in range(PAIRS):
        q, k, v = q_s[:, lanes(pair)], k_s[:, lanes(pair)], v_s[:, lanes(pair)]
        sp = mm_t(stack(q), k) * p_s[pair]
        sp_s[pair] = sp
        weights = sp.astype(BF16)
        v_2 = stack(v)
        loc_s[pair] = mm(weights[:TOK], v_2[:TOK]) + mm(weights[TOK:], v_2[TOK:])

    state = jnp.zeros((ROWS, LANES), F32)
    for there in range(CHIPS - 1):

        @pl.when(z != there)
        def _():
            from_chip(0, send1.at[there, pl.ds(0, SENT)], recv1.at[:, pl.ds(0, SENT)], there).wait_recv()

        state = recv1[there, ROWS : ROWS + 1, :] * state + recv1[there, :ROWS, :]
        send2[there + 1] = state
    for step in FAR_FIRST:
        there = lax.rem(z + step, CHIPS)

        @pl.when(there != 0)
        def _():
            to_chip(1, send2.at[there], recv2, there).start()

    @pl.when(z != 0)
    def _():
        recv2[z] = send2[z]

    @pl.when(z == 0)
    def _():
        recv2[...] = jnp.zeros_like(recv2)

    for pair in range(PAIRS):
        q, k = q_s[:, lanes(pair)], k_s[:, lanes(pair)]
        spt_s[pair] = mm_t(stack(k), q) * pt_s[pair]
        qet_s[pair] = (q.astype(F32) * entry_s[pair]).T.astype(BF16)

    def wait_slices(phase, pair, source, target):
        for i in range(4):
            there = pair * 4 + i

            @pl.when((there != z) & (z != unsent[phase]))
            def _():
                from_chip(phase, source.at[there], target, there).wait_recv()

    in_swaps = []
    for i, pair in enumerate(near_pairs):
        wait_slices(1, pair, send2, recv2)
        index = MINE * core + pair
        s_0, _ = in_order(st_own[index], st_oth[pair])
        c_0, _ = carries(pair)
        arrived = recv2[pl.ds(pair * 4, 4)].reshape(HALF, LANES)
        own, other = in_order(arrived, c_0 * arrived + s_0)
        si_s[index] = own
        si_x[pair] = other
        in_swaps.append(to_partner(si_x.at[pair], si_s.at[index], 5 + i))
        in_swaps[-1].start()

    mean_of = jnp.where((row_i < HALF) == low, 1.0 / HALF, 0.0).astype(BF16)
    def mix(pair):
        q = q_s[:, lanes(pair)]
        gain = gain_ref[pl.ds(pair, 1), :]
        carried = entry_s[pair] * mm(q, block_diagonal(si_s[pair]).astype(BF16))
        car_s[pair] = carried
        mixture = loc_s[pair] + carried
        up = u_s[:, lanes(pair)].astype(F32)
        grad = up * gain
        square = split_mm(mixture * mixture, mean_of)
        product = split_mm(grad * mixture, mean_of)
        inverse = lax.rsqrt(square + EPSILON)
        normed = mixture * inverse
        mixed = (inverse * (grad - normed * (inverse * product))).astype(BF16)
        out_ref[:, lanes(pair)] = (normed * gain).astype(BF16)
        gain_own[pl.ds(pair, 1), :] = jnp.sum(up * normed, axis=0, keepdims=True)
        g_s[pair] = mixed
        qs_own[pair] = compact(mm(qet_s[pair], mixed))

    for pair in range(MINE):
        mix(MINE * core + pair)
    for swap in in_swaps:
        swap.wait_recv()
    for pair in range(MINE):
        mix(MINE * (1 - core) + pair)

    query_swaps = [to_partner(qs_own.at[MINE * (1 - core) + pair], qs_oth.at[pair], 9 + i) for i, pair in enumerate(far_pairs)]
    gain_swap = to_partner(gain_own, gain_oth, 13)
    for swap in query_swaps:
        swap.start()
    gain_swap.start()
    for pair, swap in zip(far_pairs, query_swaps):
        swap.wait_recv()
        s_0, s_1 = in_order(qs_own[MINE * core + pair], qs_oth[pair])
        c_0, _ = carries(pair)
        send3[pl.ds(pair * 4, 4)] = (s_0 + c_0 * s_1).reshape(4, ROWS, LANES)
        start_slices(2, pair, send3, recv3)
    recv3[z] = send3[z]

    places = (lax.rem(dp, 4), dp // 4, lax.rem(z, 4), group)

    def gain_copies(level, arriving):
        copies = []
        for step in range(1, 4):
            if level == 0:
                target = {"dp": row_peer(dp, step)}
            elif level == 1:
                target = {"dp": column_peer(dp, step)}
            elif level == 2:
                target = {"seq": chip(group * 4 + lax.rem(z + step, 4))}
            else:
                target = {"seq": chip(lax.rem(z + 4 * step, CHIPS))}
            there = lax.rem(places[level] + step, 4)
            slot = there if arriving else places[level]
            copies.append(
                pltpu.make_async_remote_copy(
                    gain_out.at[level], gain_in.at[level, slot], g_send.at[level, there], g_recv.at[level, slot],
                    device_id=target, device_id_type=MESH,
                )
            )
        return copies

    def send_gain(level, value):
        gain_out[level] = value
        gain_in[level, places[level]] = value
        for copy in gain_copies(level, False):
            copy.start()

    def gain_arrived(level):
        for copy in gain_copies(level, True):
            copy.wait_recv()
        return jnp.sum(gain_in[level], axis=0)

    gain_swap.wait_recv()
    send_gain(0, gain_own[...] + gain_oth[...])

    head_i = lax.broadcasted_iota(jnp.int32, (LANES, HEADS), 1)
    half_i = (lax.broadcasted_iota(jnp.int32, (LANES, HEADS), 0) >= HALF).astype(jnp.int32)
    column_i = lax.broadcasted_iota(jnp.int32, (TOK, HEADS), 1)

    def head_of(pair):
        return (head_i == 2 * pair + half_i).astype(BF16)

    later = jnp.zeros((TOK, HEADS), F32)
    for pair in range(PAIRS):
        if pair == MINE:
            send_gain(1, gain_arrived(0))
        q, k, v = q_s[:, lanes(pair)], k_s[:, lanes(pair)], v_s[:, lanes(pair)]
        mixed = g_s[pair]
        pairs = mm_t(stack(mixed), v)
        grad_weights = (pairs * p_s[pair]).astype(BF16)
        k_2 = stack(k)
        query_state = block_diagonal(si_s[pair]).astype(BF16)
        dq = mm(grad_weights[:TOK], k_2[:TOK]) + mm(grad_weights[TOK:], k_2[TOK:]) + entry_s[pair] * mm_t(mixed, query_state)
        dq_ref[:, lanes(pair)] = dq.astype(BF16)
        pairs_t = mm_t(stack(v), mixed)
        grad_weights_t = (pairs_t * pt_s[pair]).astype(BF16)
        q_2 = stack(q)
        dkl_s[pair] = mm(grad_weights_t[:TOK], q_2[:TOK]) + mm(grad_weights_t[TOK:], q_2[TOK:])
        weights_t = spt_s[pair].astype(BF16)
        g_2 = stack(mixed)
        dvl_s[pair] = mm(weights_t[:TOK], g_2[:TOK]) + mm(weights_t[TOK:], g_2[TOK:])
        balance = jnp.sum(sp_s[pair] * pairs - spt_s[pair] * pairs_t, axis=1, keepdims=True)
        later = later + jnp.where(column_i == 2 * pair, balance[:TOK], 0.0)
        later = later + jnp.where(column_i == 2 * pair + 1, balance[TOK:], 0.0)
        later = later + split_mm(car_s[pair] * mixed.astype(F32), head_of(pair))

    send_gain(2, gain_arrived(1))

    state = jnp.zeros((ROWS, LANES), F32)
    for there in reversed(range(1, CHIPS)):

        @pl.when(z != there)
        def _():
            from_chip(2, send3.at[there], recv3, there).wait_recv()

        state = recv3[there] if there == CHIPS - 1 else recv1[there, ROWS : ROWS + 1, :] * state + recv3[there]
        send4[there - 1] = state
    for there in range(CHIPS - 1):

        @pl.when(z != there)
        def _():
            to_chip(3, send4.at[there], recv4, there).start()

    @pl.when(z != CHIPS - 1)
    def _():
        recv4[z] = send4[z]

    @pl.when(z == CHIPS - 1)
    def _():
        recv4[...] = jnp.zeros_like(recv4)

    send_gain(3, gain_arrived(2))

    later_sum = split_mm_left((row_i <= col_i).astype(BF16), later)

    grad_swaps = []
    for i, pair in enumerate(near_pairs):
        wait_slices(3, pair, send4, recv4)
        index = MINE * core + pair
        _, s_1 = in_order(qs_own[index], qs_oth[pair])
        _, c_1 = carries(pair)
        arrived = recv4[pl.ds(pair * 4, 4)].reshape(HALF, LANES)
        own, other = in_order(s_1 + c_1 * arrived, arrived)
        sg_s[index] = own
        sg_x[pair] = other
        grad_swaps.append(to_partner(sg_x.at[pair], sg_s.at[index], 14 + i))
        grad_swaps[-1].start()

    earlier = jnp.zeros((TOK + 8, HEADS), F32)

    def finish(pair, earlier):
        k, v = k_s[:, lanes(pair)], v_s[:, lanes(pair)]
        state_grad = block_diagonal(sg_s[pair]).astype(BF16)
        dk_ref[:, lanes(pair)] = (dkl_s[pair] + exit_s[pair] * mm_t(v, state_grad)).astype(BF16)
        carried_value = exit_s[pair] * mm(k, state_grad)
        dv_ref[:, lanes(pair)] = (dvl_s[pair] + carried_value).astype(BF16)
        through = jnp.sum(si_s[pair] * sg_s[pair], axis=0, keepdims=True) * carr_own[pl.ds(pair, 1), :]
        terms = jnp.concatenate([carried_value * v.astype(F32), jnp.broadcast_to(through, (8, LANES))], axis=0)
        return earlier + split_mm(terms, head_of(pair))

    for pair in range(MINE):
        earlier = finish(MINE * core + pair, earlier)
    for swap in grad_swaps:
        swap.wait_recv()
    for pair in range(MINE):
        earlier = finish(MINE * (1 - core) + pair, earlier)
    total = later_sum + split_mm_left((row_i > col_i).astype(BF16), earlier[:TOK]) + earlier[TOK : TOK + 1]
    dd_ref[...] = total.T
    dg_ref[...] = gain_arrived(3)

    for swap in (carry_swap, gain_swap, *state_swaps, *in_swaps, *query_swaps, *grad_swaps):
        swap.wait_send()
    for step in range(1, CHIPS):
        there = lax.rem(z + step, CHIPS)
        copies = (
            to_chip(0, send1.at[there, pl.ds(0, SENT)], recv1.at[:, pl.ds(0, SENT)], there),
            to_chip(1, send2.at[there], recv2, there),
            to_chip(2, send3.at[there], recv3, there),
            to_chip(3, send4.at[there], recv4, there),
        )
        for phase, copy in enumerate(copies):

            @pl.when((there if phase % 2 else z) != unsent[phase])
            def _(copy=copy):
                copy.wait_send()

    for level in range(4):
        for copy in gain_copies(level, False):
            copy.wait_send()


def write_out(*refs):
    sources, targets, sem = refs[:6], refs[6:12], refs[12]
    copies = [pltpu.make_async_copy(source, target, sem.at[i]) for i, (source, target) in enumerate(zip(sources, targets))]
    for copy in copies:
        copy.start()
    for copy in copies:
        copy.wait()


def local(queries, key_vectors, value_vectors, log_decay, restart, norm_gain, upstream):
    width = queries.shape[-1]
    vmem = pl.BlockSpec(memory_space=pltpu.VMEM)
    hbm = pl.BlockSpec(memory_space=pltpu.HBM)
    wide = pltpu.VMEM((TOK, width), BF16)
    table = pltpu.VMEM((PAIRS, TOK, LANES), F32)
    table_bf16 = pltpu.VMEM((PAIRS, TOK, LANES), BF16)
    double = pltpu.VMEM((PAIRS, 2 * TOK, LANES), F32)
    states = pltpu.VMEM((PAIRS, HALF, LANES), F32)
    some_states = pltpu.VMEM((MINE, HALF, LANES), F32)
    tile = pltpu.VMEM((8, LANES), F32)
    slices = pltpu.VMEM((CHIPS, ROWS, LANES), F32)
    slices_and = pltpu.VMEM((CHIPS, ROWS + 8, LANES), F32)
    dma = pltpu.SemaphoreType.DMA
    rows = jax.ShapeDtypeStruct((TOK, width), BF16)
    results = (
        rows, rows, rows, rows,
        jax.ShapeDtypeStruct((HEADS, TOK), F32),
        jax.ShapeDtypeStruct((8, LANES), F32),
    )
    outs = pl.pallas_call(
        kernel,
        out_shape=results,
        in_specs=[hbm] * 7,
        out_specs=[vmem] * 6,
        scratch_shapes=[
            wide, wide, wide, wide,
            pltpu.VMEM((HEADS, TOK), F32), pltpu.VMEM((1, TOK), jnp.int32), tile, dma((7,)),
            table, table, double, double, double, double, table, table, table_bf16, table_bf16, table, table,
            states, some_states, states, some_states, tile, tile, states, some_states, states, some_states,
            slices_and, slices_and, slices, slices, slices, slices, slices, slices,
            tile, tile, pltpu.VMEM((4, 8, LANES), F32), pltpu.VMEM((4, 4, 8, LANES), F32),
            dma((18,)), dma((18,)), dma((4, CHIPS)), dma((4, CHIPS)), dma((4, 4)), dma((4, 4)),
        ],
        compiler_params=pltpu.CompilerParams(collective_id=0, has_side_effects=True, vmem_limit_bytes=32 * 1024 * 1024),
    )(
        *(
            pltpu.with_memory_space_constraint(array, pltpu.HBM)
            for array in (
                queries[0], key_vectors[0], value_vectors[0], upstream[0],
                log_decay[0].T, restart, norm_gain.reshape(8, LANES),
            )
        )
    )
    layer_out, dq, dk, dv, dd, dg = pl.pallas_call(
        write_out,
        out_shape=tuple(pltpu.HBM(result.shape, result.dtype) for result in results),
        in_specs=[vmem] * 6,
        out_specs=[hbm] * 6,
        scratch_shapes=[dma((6,))],
    )(*(pltpu.with_memory_space_constraint(array, pltpu.VMEM) for array in outs))
    return (layer_out[None], dq[None], dk[None], dv[None], dd.T[None], dg.reshape(-1))


def solution(mesh):
    row, narrow = P("dp", "seq", None), P("dp", "seq")
    return jax.shard_map(
        local,
        mesh=mesh,
        in_specs=(row, row, row, row, narrow, P(), row),
        out_specs=(row, row, row, row, row, P()),
        check_vma=False,
    )
```

```python
import functools

import jax
import jax.numpy as jnp
from jax import lax
from jax.experimental import pallas as pl
from jax.experimental.pallas import tpu as pltpu
from jax.sharding import PartitionSpec as P

MESH = pl.DeviceIdType.MESH
HEADS = 16
PAIRS = HEADS // 2
MINE = PAIRS // 2
TOK = 128
LANES = 128
HALF = 64
CHIPS = 16
ROWS = MINE * HALF // CHIPS
SENT = ROWS + 1
EPSILON = 1e-06
F32 = jnp.float32
BF16 = jnp.bfloat16
FAR_FIRST = (8, 7, 9, 6, 10, 5, 11, 4, 12, 3, 13, 2, 14, 1, 15)


def mm(a, b):
    return jnp.dot(a, b, preferred_element_type=F32)


def mm_t(a, b):
    return lax.dot_general(a, b, (((1,), (1,)), ((), ())), preferred_element_type=F32)


def t_mm(a, b):
    return lax.dot_general(a, b, (((0,), (0,)), ((), ())), preferred_element_type=F32)


def split_mm(a, b):
    high = a.astype(BF16)
    low = (a - high.astype(F32)).astype(BF16)
    return mm(high, b) + mm(low, b)


def split_t_mm(a, b):
    high = a.astype(BF16)
    low = (a - high.astype(F32)).astype(BF16)
    return t_mm(high, b) + t_mm(low, b)


def split_mm_left(a, b):
    high = b.astype(BF16)
    low = (b - high.astype(F32)).astype(BF16)
    return mm(a, high) + mm(a, low)


def row_peer(dp, step):
    return dp // 4 * 4 + lax.rem(dp + step, 4)


def column_peer(dp, step):
    return lax.rem(dp + 4 * step, 16)


def kernel(
    q_hbm, k_hbm, v_hbm, u_hbm, ld_hbm, rs_hbm, gain_hbm,
    out_ref, dq_ref, dk_ref, dv_ref, dd_ref, dg_ref,
    q_s, k_s, v_s, u_s, ld_ref, rs_ref, gain_ref, in_sem,
    entry_s, exit_s, p_s, pt_s, sp_s, spt_s, loc_s, car_s, qet_s, qetl_s, g_s, dkl_s, dvl_s,
    st_own, st_oth, qs_own, qs_oth, carr_own, carr_oth, si_s, si_x, sg_s, sg_x,
    send1, recv1, send2, recv2, send3, recv3, send4, recv4,
    gain_own, gain_oth, gain_out, gain_in,
    x_send, x_recv, p_send, p_recv, g_send, g_recv,
):
    seq = lax.axis_index("seq")
    dp = lax.axis_index("dp")
    z = seq // 2
    core = lax.rem(seq, 2)
    partner = z * 2 + (1 - core)

    def chip(index):
        return index * 2 + core

    loads = [
        pltpu.make_async_copy(source, target, in_sem.at[i])
        for i, (source, target) in enumerate(
            ((ld_hbm, ld_ref), (rs_hbm, rs_ref), (k_hbm, k_s), (v_hbm, v_s), (q_hbm, q_s), (u_hbm, u_s), (gain_hbm, gain_ref))
        )
    ]
    for load in loads:
        load.start()

    barrier = pltpu.get_barrier_semaphore()
    for step in FAR_FIRST:
        pl.semaphore_signal(barrier, inc=1, device_id={"seq": chip(lax.rem(z + step, CHIPS))}, device_id_type=MESH)
    for step in range(1, 4):
        for there in (row_peer(dp, step), column_peer(dp, step)):
            pl.semaphore_signal(barrier, inc=1, device_id={"dp": there}, device_id_type=MESH)
    pl.semaphore_signal(barrier, inc=1, device_id={"seq": partner}, device_id_type=MESH)

    def lanes(pair):
        if isinstance(pair, int):
            return slice(pair * LANES, (pair + 1) * LANES)
        return pl.ds(pl.multiple_of(pair * LANES, LANES), LANES)

    row_i = lax.broadcasted_iota(jnp.int32, (TOK, TOK), 0)
    col_i = lax.broadcasted_iota(jnp.int32, (TOK, TOK), 1)
    low = col_i < HALF
    low_half = low[:HALF]
    tri = row_i >= col_i

    def both(column_a, column_b):
        return jnp.where(low, column_a, column_b)

    def stack(x):
        zero = jnp.zeros_like(x)
        return jnp.concatenate([jnp.where(low, x, zero), jnp.where(low, zero, x)], axis=0)

    def compact(x):
        return jnp.where(low_half, x[:HALF], x[HALF:])

    def block_diagonal(x):
        zero = jnp.zeros_like(x)
        return jnp.concatenate([jnp.where(low_half, x, zero), jnp.where(low_half, zero, x)], axis=0)

    loads[0].wait()
    loads[1].wait()
    marks = rs_ref[...].astype(F32)
    resets_col = jnp.sum(jnp.where(tri, marks, 0.0), axis=1, keepdims=True)
    resets_row = mm(jnp.broadcast_to(marks, (8, TOK)).astype(BF16), (row_i <= col_i).astype(BF16))[0:1]
    last_reset = resets_row[:, TOK - 1 :]
    cum_t = jnp.dot(
        ld_ref[...], (row_i <= col_i).astype(F32), precision=lax.Precision.HIGHEST, preferred_element_type=F32
    )
    cum = cum_t.T
    last_total = cum[TOK - 1 :, :]
    exit_all = jnp.where(resets_col == last_reset, jnp.exp(last_total - cum), 0.0)
    carry_all = jnp.where(last_reset == 0.0, jnp.exp(last_total), 0.0)
    for pair in range(PAIRS):
        a, b = 2 * pair, 2 * pair + 1
        exit_s[pair] = both(exit_all[:, a : a + 1], exit_all[:, b : b + 1])
        carr_own[pair : pair + 1, :] = jnp.where(low[0:1], carry_all[:, a : a + 1], carry_all[:, b : b + 1])

    loads[2].wait()
    loads[3].wait()
    for pair in range(PAIRS):
        decayed = k_s[:, lanes(pair)].astype(F32) * exit_s[pair]
        st_own[pair] = compact(split_t_mm(decayed, v_s[:, lanes(pair)]))

    pl.semaphore_wait(barrier, 22)

    group = z // 4
    far_pairs = [lax.rem(group + step, 4) for step in (2, 1, 3, 0)]
    near_pairs = far_pairs[::-1]

    def to_partner(source, target, index):
        return pltpu.make_async_remote_copy(
            source, target, x_send.at[index], x_recv.at[index], device_id={"seq": partner}, device_id_type=MESH
        )

    def to_chip(phase, source, target, there):
        return pltpu.make_async_remote_copy(
            source, target.at[z], p_send.at[phase, there], p_recv.at[phase, z],
            device_id={"seq": chip(there)}, device_id_type=MESH,
        )

    def from_chip(phase, source, target, there):
        return pltpu.make_async_remote_copy(
            source, target.at[there], p_send.at[phase, there], p_recv.at[phase, there],
            device_id={"seq": chip(there)}, device_id_type=MESH,
        )

    first = core == 0

    def in_order(own, other):
        return jnp.where(first, own, other), jnp.where(first, other, own)

    carry_swap = to_partner(carr_own, carr_oth, 0)
    state_swaps = [to_partner(st_own.at[MINE * (1 - core) + pair], st_oth.at[pair], 1 + i) for i, pair in enumerate(far_pairs)]
    carry_swap.start()
    for swap in state_swaps:
        swap.start()
    carry_swap.wait_recv()

    def carries(pair):
        index = pl.ds(MINE * core + pair, 1)
        return in_order(carr_own[index, :], carr_oth[index, :])

    unsent = (CHIPS - 1, 0, 0, CHIPS - 1)

    def start_slices(phase, pair, source, target):
        for i in range(4):
            there = pair * 4 + i

            @pl.when((there != z) & (z != unsent[phase]))
            def _():
                to_chip(phase, source.at[there], target, there).start()

    for pair, swap in zip(far_pairs, state_swaps):
        swap.wait_recv()
        s_0, s_1 = in_order(st_own[MINE * core + pair], st_oth[pair])
        c_0, c_1 = carries(pair)
        send1[pl.ds(pair * 4, 4), :ROWS, :] = (c_1 * s_0 + s_1).reshape(4, ROWS, LANES)
        send1[pl.ds(pair * 4, 4), ROWS:, :] = jnp.broadcast_to(c_0 * c_1, (4, 8, LANES))
        start_slices(0, pair, send1.at[:, pl.ds(0, SENT)], recv1.at[:, pl.ds(0, SENT)])
    recv1[z] = send1[z]

    entry_all = jnp.where(resets_col == 0.0, jnp.exp(cum), 0.0)
    same = resets_col == resets_row
    allowed = tri & same
    allowed_t = (row_i <= col_i) & same
    for head in range(HEADS):
        column, row = cum[:, head : head + 1], cum_t[head : head + 1, :]
        spread = column - row
        rows = slice((head % 2) * TOK, (head % 2 + 1) * TOK)
        p_s[head // 2, rows] = jnp.exp(jnp.where(allowed, spread, -1e30))
        pt_s[head // 2, rows] = jnp.exp(jnp.where(allowed_t, -spread, -1e30))
    for pair in range(PAIRS):
        a, b = 2 * pair, 2 * pair + 1
        entry_s[pair] = both(entry_all[:, a : a + 1], entry_all[:, b : b + 1])
    loads[4].wait()
    loads[5].wait()
    loads[6].wait()
    for pair in range(PAIRS):
        q, k, v = q_s[:, lanes(pair)], k_s[:, lanes(pair)], v_s[:, lanes(pair)]
        sp = mm_t(stack(q), k) * p_s[pair]
        sp_s[pair] = sp
        weights = sp.astype(BF16)
        v_2 = stack(v)
        loc_s[pair] = mm(weights[:TOK], v_2[:TOK]) + mm(weights[TOK:], v_2[TOK:])

    for pair in range(PAIRS):
        q, k = q_s[:, lanes(pair)], k_s[:, lanes(pair)]
        spt_s[pair] = mm_t(stack(k), q) * pt_s[pair]
        decayed = (q.astype(F32) * entry_s[pair]).T
        qet_s[pair] = decayed.astype(BF16)
        qetl_s[pair] = (decayed - decayed.astype(BF16).astype(F32)).astype(BF16)

    state = jnp.zeros((ROWS, LANES), F32)
    for there in range(CHIPS - 1):

        @pl.when(z != there)
        def _():
            from_chip(0, send1.at[there, pl.ds(0, SENT)], recv1.at[:, pl.ds(0, SENT)], there).wait_recv()

        state = recv1[there, ROWS : ROWS + 1, :] * state + recv1[there, :ROWS, :]
        send2[there + 1] = state
    for step in FAR_FIRST:
        there = lax.rem(z + step, CHIPS)

        @pl.when(there != 0)
        def _():
            to_chip(1, send2.at[there], recv2, there).start()

    @pl.when(z != 0)
    def _():
        recv2[z] = send2[z]

    @pl.when(z == 0)
    def _():
        recv2[...] = jnp.zeros_like(recv2)

    def wait_slices(phase, pair, source, target):
        for i in range(4):
            there = pair * 4 + i

            @pl.when((there != z) & (z != unsent[phase]))
            def _():
                from_chip(phase, source.at[there], target, there).wait_recv()

    in_swaps = []
    for i, pair in enumerate(near_pairs):
        wait_slices(1, pair, send2, recv2)
        index = MINE * core + pair
        s_0, _ = in_order(st_own[index], st_oth[pair])
        c_0, _ = carries(pair)
        arrived = recv2[pl.ds(pair * 4, 4)].reshape(HALF, LANES)
        own, other = in_order(arrived, c_0 * arrived + s_0)
        si_s[index] = own
        si_x[pair] = other
        in_swaps.append(to_partner(si_x.at[pair], si_s.at[index], 5 + i))
        in_swaps[-1].start()

    mean_of = jnp.where((row_i < HALF) == low, 1.0 / HALF, 0.0).astype(BF16)
    def mix(pair):
        q = q_s[:, lanes(pair)]
        gain = gain_ref[pl.ds(pair, 1), :]
        carried = entry_s[pair] * split_mm_left(q, block_diagonal(si_s[pair]))
        car_s[pair] = carried
        mixture = loc_s[pair] + carried
        up = u_s[:, lanes(pair)].astype(F32)
        grad = up * gain
        square = split_mm(mixture * mixture, mean_of)
        product = split_mm(grad * mixture, mean_of)
        inverse = lax.rsqrt(square + EPSILON)
        normed = mixture * inverse
        mixed = (inverse * (grad - normed * (inverse * product))).astype(BF16)
        out_ref[:, lanes(pair)] = (normed * gain).astype(BF16)
        gain_own[pl.ds(pair, 1), :] = jnp.sum(up * normed, axis=0, keepdims=True)
        g_s[pair] = mixed
        qs_own[pair] = compact(mm(qet_s[pair], mixed) + mm(qetl_s[pair], mixed))

    for pair in range(MINE):
        mix(MINE * core + pair)
    for swap in in_swaps:
        swap.wait_recv()
    for pair in range(MINE):
        mix(MINE * (1 - core) + pair)

    query_swaps = [to_partner(qs_own.at[MINE * (1 - core) + pair], qs_oth.at[pair], 9 + i) for i, pair in enumerate(far_pairs)]
    gain_swap = to_partner(gain_own, gain_oth, 13)
    for swap in query_swaps:
        swap.start()
    gain_swap.start()
    for pair, swap in zip(far_pairs, query_swaps):
        swap.wait_recv()
        s_0, s_1 = in_order(qs_own[MINE * core + pair], qs_oth[pair])
        c_0, _ = carries(pair)
        send3[pl.ds(pair * 4, 4)] = (s_0 + c_0 * s_1).reshape(4, ROWS, LANES)
        start_slices(2, pair, send3, recv3)
    recv3[z] = send3[z]

    places = (lax.rem(dp, 4), dp // 4, lax.rem(z, 4), group)

    def gain_copies(level, arriving):
        copies = []
        for step in range(1, 4):
            if level == 0:
                target = {"dp": row_peer(dp, step)}
            elif level == 1:
                target = {"dp": column_peer(dp, step)}
            elif level == 2:
                target = {"seq": chip(group * 4 + lax.rem(z + step, 4))}
            else:
                target = {"seq": chip(lax.rem(z + 4 * step, CHIPS))}
            there = lax.rem(places[level] + step, 4)
            slot = there if arriving else places[level]
            copies.append(
                pltpu.make_async_remote_copy(
                    gain_out.at[level], gain_in.at[level, slot], g_send.at[level, there], g_recv.at[level, slot],
                    device_id=target, device_id_type=MESH,
                )
            )
        return copies

    def send_gain(level, value):
        gain_out[level] = value
        gain_in[level, places[level]] = value
        for copy in gain_copies(level, False):
            copy.start()

    def gain_arrived(level):
        for copy in gain_copies(level, True):
            copy.wait_recv()
        return jnp.sum(gain_in[level], axis=0)

    gain_swap.wait_recv()
    send_gain(0, gain_own[...] + gain_oth[...])

    head_i = lax.broadcasted_iota(jnp.int32, (LANES, HEADS), 1)
    half_i = (lax.broadcasted_iota(jnp.int32, (LANES, HEADS), 0) >= HALF).astype(jnp.int32)
    column_i = lax.broadcasted_iota(jnp.int32, (TOK, HEADS), 1)

    def head_of(pair):
        return (head_i == 2 * pair + half_i).astype(BF16)

    later = jnp.zeros((TOK, HEADS), F32)
    for pair in range(PAIRS):
        if pair == MINE:
            send_gain(1, gain_arrived(0))
        q, k, v = q_s[:, lanes(pair)], k_s[:, lanes(pair)], v_s[:, lanes(pair)]
        mixed = g_s[pair]
        pairs = mm_t(stack(mixed), v)
        grad_weights = (pairs * p_s[pair]).astype(BF16)
        k_2 = stack(k)
        query_state = block_diagonal(si_s[pair]).astype(BF16)
        dq = mm(grad_weights[:TOK], k_2[:TOK]) + mm(grad_weights[TOK:], k_2[TOK:]) + entry_s[pair] * mm_t(mixed, query_state)
        dq_ref[:, lanes(pair)] = dq.astype(BF16)
        pairs_t = mm_t(stack(v), mixed)
        grad_weights_t = (pairs_t * pt_s[pair]).astype(BF16)
        q_2 = stack(q)
        dkl_s[pair] = mm(grad_weights_t[:TOK], q_2[:TOK]) + mm(grad_weights_t[TOK:], q_2[TOK:])
        weights_t = spt_s[pair].astype(BF16)
        g_2 = stack(mixed)
        dvl_s[pair] = mm(weights_t[:TOK], g_2[:TOK]) + mm(weights_t[TOK:], g_2[TOK:])
        balance = jnp.sum(sp_s[pair] * pairs - spt_s[pair] * pairs_t, axis=1, keepdims=True)
        later = later + jnp.where(column_i == 2 * pair, balance[:TOK], 0.0)
        later = later + jnp.where(column_i == 2 * pair + 1, balance[TOK:], 0.0)
        later = later + split_mm(car_s[pair] * mixed.astype(F32), head_of(pair))

    send_gain(2, gain_arrived(1))

    state = jnp.zeros((ROWS, LANES), F32)
    for there in reversed(range(1, CHIPS)):

        @pl.when(z != there)
        def _():
            from_chip(2, send3.at[there], recv3, there).wait_recv()

        state = recv3[there] if there == CHIPS - 1 else recv1[there, ROWS : ROWS + 1, :] * state + recv3[there]
        send4[there - 1] = state
    for there in range(CHIPS - 1):

        @pl.when(z != there)
        def _():
            to_chip(3, send4.at[there], recv4, there).start()

    @pl.when(z != CHIPS - 1)
    def _():
        recv4[z] = send4[z]

    @pl.when(z == CHIPS - 1)
    def _():
        recv4[...] = jnp.zeros_like(recv4)

    send_gain(3, gain_arrived(2))

    later_sum = split_mm_left((row_i <= col_i).astype(BF16), later)

    grad_swaps = []
    for i, pair in enumerate(near_pairs):
        wait_slices(3, pair, send4, recv4)
        index = MINE * core + pair
        _, s_1 = in_order(qs_own[index], qs_oth[pair])
        _, c_1 = carries(pair)
        arrived = recv4[pl.ds(pair * 4, 4)].reshape(HALF, LANES)
        own, other = in_order(s_1 + c_1 * arrived, arrived)
        sg_s[index] = own
        sg_x[pair] = other
        grad_swaps.append(to_partner(sg_x.at[pair], sg_s.at[index], 14 + i))
        grad_swaps[-1].start()

    earlier = jnp.zeros((TOK + 8, HEADS), F32)

    def finish(pair, earlier):
        k, v = k_s[:, lanes(pair)], v_s[:, lanes(pair)]
        state_grad = block_diagonal(sg_s[pair])
        dk_ref[:, lanes(pair)] = (dkl_s[pair] + exit_s[pair] * mm_t(v, state_grad.astype(BF16))).astype(BF16)
        carried_value = exit_s[pair] * split_mm_left(k, state_grad)
        dv_ref[:, lanes(pair)] = (dvl_s[pair] + carried_value).astype(BF16)
        through = jnp.sum(si_s[pair] * sg_s[pair], axis=0, keepdims=True) * carr_own[pl.ds(pair, 1), :]
        terms = jnp.concatenate([carried_value * v.astype(F32), jnp.broadcast_to(through, (8, LANES))], axis=0)
        return earlier + split_mm(terms, head_of(pair))

    for pair in range(MINE):
        earlier = finish(MINE * core + pair, earlier)
    for swap in grad_swaps:
        swap.wait_recv()
    for pair in range(MINE):
        earlier = finish(MINE * (1 - core) + pair, earlier)
    total = later_sum + split_mm_left((row_i > col_i).astype(BF16), earlier[:TOK]) + earlier[TOK : TOK + 1]
    dd_ref[...] = total.T
    dg_ref[...] = gain_arrived(3)

    for swap in (carry_swap, gain_swap, *state_swaps, *in_swaps, *query_swaps, *grad_swaps):
        swap.wait_send()
    for step in range(1, CHIPS):
        there = lax.rem(z + step, CHIPS)
        copies = (
            to_chip(0, send1.at[there, pl.ds(0, SENT)], recv1.at[:, pl.ds(0, SENT)], there),
            to_chip(1, send2.at[there], recv2, there),
            to_chip(2, send3.at[there], recv3, there),
            to_chip(3, send4.at[there], recv4, there),
        )
        for phase, copy in enumerate(copies):

            @pl.when((there if phase % 2 else z) != unsent[phase])
            def _(copy=copy):
                copy.wait_send()

    for level in range(4):
        for copy in gain_copies(level, False):
            copy.wait_send()


def write_out(*refs):
    sources, targets, sem = refs[:6], refs[6:12], refs[12]
    copies = [pltpu.make_async_copy(source, target, sem.at[i]) for i, (source, target) in enumerate(zip(sources, targets))]
    for copy in copies:
        copy.start()
    for copy in copies:
        copy.wait()


def local(queries, key_vectors, value_vectors, log_decay, restart, norm_gain, upstream):
    width = queries.shape[-1]
    vmem = pl.BlockSpec(memory_space=pltpu.VMEM)
    hbm = pl.BlockSpec(memory_space=pltpu.HBM)
    wide = pltpu.VMEM((TOK, width), BF16)
    table = pltpu.VMEM((PAIRS, TOK, LANES), F32)
    table_bf16 = pltpu.VMEM((PAIRS, TOK, LANES), BF16)
    double = pltpu.VMEM((PAIRS, 2 * TOK, LANES), F32)
    states = pltpu.VMEM((PAIRS, HALF, LANES), F32)
    some_states = pltpu.VMEM((MINE, HALF, LANES), F32)
    tile = pltpu.VMEM((8, LANES), F32)
    slices = pltpu.VMEM((CHIPS, ROWS, LANES), F32)
    slices_and = pltpu.VMEM((CHIPS, ROWS + 8, LANES), F32)
    dma = pltpu.SemaphoreType.DMA
    rows = jax.ShapeDtypeStruct((TOK, width), BF16)
    results = (
        rows, rows, rows, rows,
        jax.ShapeDtypeStruct((HEADS, TOK), F32),
        jax.ShapeDtypeStruct((8, LANES), F32),
    )
    outs = pl.pallas_call(
        kernel,
        out_shape=results,
        in_specs=[hbm] * 7,
        out_specs=[vmem] * 6,
        scratch_shapes=[
            wide, wide, wide, wide,
            pltpu.VMEM((HEADS, TOK), F32), pltpu.VMEM((1, TOK), jnp.int32), tile, dma((7,)),
            table, table, double, double, double, double, table, table, table_bf16, table_bf16, table_bf16, table, table,
            states, some_states, states, some_states, tile, tile, states, some_states, states, some_states,
            slices_and, slices_and, slices, slices, slices, slices, slices, slices,
            tile, tile, pltpu.VMEM((4, 8, LANES), F32), pltpu.VMEM((4, 4, 8, LANES), F32),
            dma((18,)), dma((18,)), dma((4, CHIPS)), dma((4, CHIPS)), dma((4, 4)), dma((4, 4)),
        ],
        compiler_params=pltpu.CompilerParams(collective_id=0, has_side_effects=True, vmem_limit_bytes=32 * 1024 * 1024),
    )(
        *(
            pltpu.with_memory_space_constraint(array, pltpu.HBM)
            for array in (
                queries[0], key_vectors[0], value_vectors[0], upstream[0],
                log_decay[0].T, restart, norm_gain.reshape(8, LANES),
            )
        )
    )
    layer_out, dq, dk, dv, dd, dg = pl.pallas_call(
        write_out,
        out_shape=tuple(pltpu.HBM(result.shape, result.dtype) for result in results),
        in_specs=[vmem] * 6,
        out_specs=[hbm] * 6,
        scratch_shapes=[dma((6,))],
    )(*(pltpu.with_memory_space_constraint(array, pltpu.VMEM) for array in outs))
    return (layer_out[None], dq[None], dk[None], dv[None], dd.T[None], dg.reshape(-1))


def solution(mesh):
    row, narrow = P("dp", "seq", None), P("dp", "seq")
    return jax.shard_map(
        local,
        mesh=mesh,
        in_specs=(row, row, row, row, narrow, P(), row),
        out_specs=(row, row, row, row, row, P()),
        check_vma=False,
    )
```

```python
import functools

import jax
import jax.numpy as jnp
from jax import lax
from jax.experimental import pallas as pl
from jax.experimental.pallas import tpu as pltpu
from jax.sharding import PartitionSpec as P

MESH = pl.DeviceIdType.MESH
HEADS = 16
PAIRS = HEADS // 2
MINE = PAIRS // 2
TOK = 128
LANES = 128
HALF = 64
CHIPS = 16
ROWS = MINE * HALF // CHIPS
SENT = ROWS + 1
EPSILON = 1e-06
F32 = jnp.float32
BF16 = jnp.bfloat16
FAR_FIRST = (8, 7, 9, 6, 10, 5, 11, 4, 12, 3, 13, 2, 14, 1, 15)


def mm(a, b):
    return jnp.dot(a, b, preferred_element_type=F32)


def mm_t(a, b):
    return lax.dot_general(a, b, (((1,), (1,)), ((), ())), preferred_element_type=F32)


def t_mm(a, b):
    return lax.dot_general(a, b, (((0,), (0,)), ((), ())), preferred_element_type=F32)


def split_mm(a, b):
    high = a.astype(BF16)
    low = (a - high.astype(F32)).astype(BF16)
    return mm(high, b) + mm(low, b)


def split_t_mm(a, b):
    high = a.astype(BF16)
    low = (a - high.astype(F32)).astype(BF16)
    return t_mm(high, b) + t_mm(low, b)


def split_mm_left(a, b):
    high = b.astype(BF16)
    low = (b - high.astype(F32)).astype(BF16)
    return mm(a, high) + mm(a, low)


def row_peer(dp, step):
    return dp // 4 * 4 + lax.rem(dp + step, 4)


def column_peer(dp, step):
    return lax.rem(dp + 4 * step, 16)


def kernel(
    q_hbm, k_hbm, v_hbm, u_hbm, ld_hbm, rs_hbm, gain_hbm,
    out_ref, dq_ref, dk_ref, dv_ref, dd_ref, dg_ref,
    q_s, k_s, v_s, u_s, ld_ref, rs_ref, gain_ref, in_sem,
    entry_s, exit_s, p_s, pt_s, sp_s, spt_s, loc_s, car_s, qet_s, qetl_s, g_s, dkl_s, dvl_s,
    st_own, st_oth, qs_own, qs_oth, carr_own, carr_oth, si_s, si_x, sg_s, sg_x,
    send1, recv1, send2, recv2, send3, recv3, send4, recv4,
    gain_own, gain_oth, gain_out, gain_in,
    x_send, x_recv, p_send, p_recv, g_send, g_recv,
):
    seq = lax.axis_index("seq")
    dp = lax.axis_index("dp")
    z = seq // 2
    core = lax.rem(seq, 2)
    partner = z * 2 + (1 - core)

    def chip(index):
        return index * 2 + core

    loads = [
        pltpu.make_async_copy(source, target, in_sem.at[i])
        for i, (source, target) in enumerate(
            ((ld_hbm, ld_ref), (rs_hbm, rs_ref), (k_hbm, k_s), (v_hbm, v_s), (q_hbm, q_s), (u_hbm, u_s), (gain_hbm, gain_ref))
        )
    ]
    for load in loads:
        load.start()

    barrier = pltpu.get_barrier_semaphore()
    for step in FAR_FIRST:
        pl.semaphore_signal(barrier, inc=1, device_id={"seq": chip(lax.rem(z + step, CHIPS))}, device_id_type=MESH)
    for step in range(1, 4):
        for there in (row_peer(dp, step), column_peer(dp, step)):
            pl.semaphore_signal(barrier, inc=1, device_id={"dp": there}, device_id_type=MESH)
    pl.semaphore_signal(barrier, inc=1, device_id={"seq": partner}, device_id_type=MESH)

    def lanes(pair):
        if isinstance(pair, int):
            return slice(pair * LANES, (pair + 1) * LANES)
        return pl.ds(pl.multiple_of(pair * LANES, LANES), LANES)

    row_i = lax.broadcasted_iota(jnp.int32, (TOK, TOK), 0)
    col_i = lax.broadcasted_iota(jnp.int32, (TOK, TOK), 1)
    low = col_i < HALF
    low_half = low[:HALF]
    tri = row_i >= col_i

    def both(column_a, column_b):
        return jnp.where(low, column_a, column_b)

    def stack(x):
        zero = jnp.zeros_like(x)
        return jnp.concatenate([jnp.where(low, x, zero), jnp.where(low, zero, x)], axis=0)

    def compact(x):
        return jnp.where(low_half, x[:HALF], x[HALF:])

    def block_diagonal(x):
        zero = jnp.zeros_like(x)
        return jnp.concatenate([jnp.where(low_half, x, zero), jnp.where(low_half, zero, x)], axis=0)

    loads[0].wait()
    loads[1].wait()
    marks = rs_ref[...].astype(F32)
    resets_col = jnp.sum(jnp.where(tri, marks, 0.0), axis=1, keepdims=True)
    resets_row = mm(jnp.broadcast_to(marks, (8, TOK)).astype(BF16), (row_i <= col_i).astype(BF16))[0:1]
    last_reset = resets_row[:, TOK - 1 :]
    cum_t = jnp.dot(
        ld_ref[...], (row_i <= col_i).astype(F32), precision=lax.Precision.HIGHEST, preferred_element_type=F32
    )
    cum = cum_t.T
    last_total = cum[TOK - 1 :, :]
    exit_all = jnp.where(resets_col == last_reset, jnp.exp(last_total - cum), 0.0)
    carry_all = jnp.where(last_reset == 0.0, jnp.exp(last_total), 0.0)
    for pair in range(PAIRS):
        a, b = 2 * pair, 2 * pair + 1
        exit_s[pair] = both(exit_all[:, a : a + 1], exit_all[:, b : b + 1])
        carr_own[pair : pair + 1, :] = jnp.where(low[0:1], carry_all[:, a : a + 1], carry_all[:, b : b + 1])

    loads[2].wait()
    loads[3].wait()
    for pair in range(PAIRS):
        decayed = k_s[:, lanes(pair)].astype(F32) * exit_s[pair]
        st_own[pair] = compact(split_t_mm(decayed, v_s[:, lanes(pair)]))

    pl.semaphore_wait(barrier, 22)

    group = z // 4
    far_pairs = [lax.rem(group + step, 4) for step in (2, 1, 3, 0)]
    near_pairs = far_pairs[::-1]

    def to_partner(source, target, index):
        return pltpu.make_async_remote_copy(
            source, target, x_send.at[index], x_recv.at[index], device_id={"seq": partner}, device_id_type=MESH
        )

    def to_chip(phase, source, target, there):
        return pltpu.make_async_remote_copy(
            source, target.at[z], p_send.at[phase, there], p_recv.at[phase, z],
            device_id={"seq": chip(there)}, device_id_type=MESH,
        )

    def from_chip(phase, source, target, there):
        return pltpu.make_async_remote_copy(
            source, target.at[there], p_send.at[phase, there], p_recv.at[phase, there],
            device_id={"seq": chip(there)}, device_id_type=MESH,
        )

    first = core == 0

    def in_order(own, other):
        return jnp.where(first, own, other), jnp.where(first, other, own)

    carry_swap = to_partner(carr_own, carr_oth, 0)
    state_swaps = [to_partner(st_own.at[MINE * (1 - core) + pair], st_oth.at[pair], 1 + i) for i, pair in enumerate(far_pairs)]
    carry_swap.start()
    for swap in state_swaps:
        swap.start()
    carry_swap.wait_recv()

    def carries(pair):
        index = pl.ds(MINE * core + pair, 1)
        return in_order(carr_own[index, :], carr_oth[index, :])

    unsent = (CHIPS - 1, 0, 0, CHIPS - 1)

    def start_slices(phase, pair, source, target):
        for i in range(4):
            there = pair * 4 + i

            @pl.when((there != z) & (z != unsent[phase]))
            def _():
                to_chip(phase, source.at[there], target, there).start()

    for pair, swap in zip(far_pairs, state_swaps):
        swap.wait_recv()
        s_0, s_1 = in_order(st_own[MINE * core + pair], st_oth[pair])
        c_0, c_1 = carries(pair)
        send1[pl.ds(pair * 4, 4), :ROWS, :] = (c_1 * s_0 + s_1).reshape(4, ROWS, LANES)
        send1[pl.ds(pair * 4, 4), ROWS:, :] = jnp.broadcast_to(c_0 * c_1, (4, 8, LANES))
        start_slices(0, pair, send1.at[:, pl.ds(0, SENT)], recv1.at[:, pl.ds(0, SENT)])
    recv1[z] = send1[z]

    entry_all = jnp.where(resets_col == 0.0, jnp.exp(cum), 0.0)
    same = resets_col == resets_row
    allowed = tri & same
    allowed_t = (row_i <= col_i) & same
    for head in range(HEADS):
        column, row = cum[:, head : head + 1], cum_t[head : head + 1, :]
        spread = column - row
        rows = slice((head % 2) * TOK, (head % 2 + 1) * TOK)
        p_s[head // 2, rows] = jnp.exp(jnp.where(allowed, spread, -1e30))
        pt_s[head // 2, rows] = jnp.exp(jnp.where(allowed_t, -spread, -1e30))
    for pair in range(PAIRS):
        a, b = 2 * pair, 2 * pair + 1
        entry_s[pair] = both(entry_all[:, a : a + 1], entry_all[:, b : b + 1])
    loads[4].wait()
    loads[5].wait()
    loads[6].wait()
    for pair in range(PAIRS):
        q, k, v = q_s[:, lanes(pair)], k_s[:, lanes(pair)], v_s[:, lanes(pair)]
        sp = mm_t(stack(q), k) * p_s[pair]
        sp_s[pair] = sp
        weights = sp.astype(BF16)
        v_2 = stack(v)
        loc_s[pair] = mm(weights[:TOK], v_2[:TOK]) + mm(weights[TOK:], v_2[TOK:])

    for pair in range(PAIRS):
        q, k = q_s[:, lanes(pair)], k_s[:, lanes(pair)]
        spt_s[pair] = mm_t(stack(k), q) * pt_s[pair]
        decayed = (q.astype(F32) * entry_s[pair]).T
        qet_s[pair] = decayed.astype(BF16)
        qetl_s[pair] = (decayed - decayed.astype(BF16).astype(F32)).astype(BF16)

    state = jnp.zeros((ROWS, LANES), F32)
    for there in range(CHIPS - 1):

        @pl.when(z != there)
        def _():
            from_chip(0, send1.at[there, pl.ds(0, SENT)], recv1.at[:, pl.ds(0, SENT)], there).wait_recv()

        state = recv1[there, ROWS : ROWS + 1, :] * state + recv1[there, :ROWS, :]
        send2[there + 1] = state
    for step in FAR_FIRST:
        there = lax.rem(z + step, CHIPS)

        @pl.when(there != 0)
        def _():
            to_chip(1, send2.at[there], recv2, there).start()

    @pl.when(z != 0)
    def _():
        recv2[z] = send2[z]

    @pl.when(z == 0)
    def _():
        recv2[...] = jnp.zeros_like(recv2)

    def wait_slices(phase, pair, source, target):
        for i in range(4):
            there = pair * 4 + i

            @pl.when((there != z) & (z != unsent[phase]))
            def _():
                from_chip(phase, source.at[there], target, there).wait_recv()

    in_swaps = []
    for i, pair in enumerate(near_pairs):
        wait_slices(1, pair, send2, recv2)
        index = MINE * core + pair
        s_0, _ = in_order(st_own[index], st_oth[pair])
        c_0, _ = carries(pair)
        arrived = recv2[pl.ds(pair * 4, 4)].reshape(HALF, LANES)
        own, other = in_order(arrived, c_0 * arrived + s_0)
        si_s[index] = own
        si_x[pair] = other
        in_swaps.append(to_partner(si_x.at[pair], si_s.at[index], 5 + i))
        in_swaps[-1].start()

    mean_of = jnp.where((row_i < HALF) == low, 1.0 / HALF, 0.0).astype(BF16)
    def mix(pair):
        q = q_s[:, lanes(pair)]
        gain = gain_ref[pl.ds(pair, 1), :]
        carried = entry_s[pair] * split_mm_left(q, block_diagonal(si_s[pair]))
        car_s[pair] = carried
        mixture = loc_s[pair] + carried
        up = u_s[:, lanes(pair)].astype(F32)
        grad = up * gain
        square = split_mm(mixture * mixture, mean_of)
        product = split_mm(grad * mixture, mean_of)
        inverse = lax.rsqrt(square + EPSILON)
        normed = mixture * inverse
        mixed = (inverse * (grad - normed * (inverse * product))).astype(BF16)
        out_ref[:, lanes(pair)] = (normed * gain).astype(BF16)
        gain_own[pl.ds(pair, 1), :] = jnp.sum(up * normed, axis=0, keepdims=True)
        g_s[pair] = mixed
        qs_own[pair] = compact(mm(qet_s[pair], mixed) + mm(qetl_s[pair], mixed))

    for pair in range(MINE):
        mix(MINE * core + pair)
    for swap in in_swaps:
        swap.wait_recv()
    for pair in range(MINE):
        mix(MINE * (1 - core) + pair)

    query_swaps = [to_partner(qs_own.at[MINE * (1 - core) + pair], qs_oth.at[pair], 9 + i) for i, pair in enumerate(far_pairs)]
    gain_swap = to_partner(gain_own, gain_oth, 13)
    for swap in query_swaps:
        swap.start()
    gain_swap.start()
    for pair, swap in zip(far_pairs, query_swaps):
        swap.wait_recv()
        s_0, s_1 = in_order(qs_own[MINE * core + pair], qs_oth[pair])
        c_0, _ = carries(pair)
        send3[pl.ds(pair * 4, 4)] = (s_0 + c_0 * s_1).reshape(4, ROWS, LANES)
        start_slices(2, pair, send3, recv3)
    recv3[z] = send3[z]

    places = (lax.rem(dp, 4), dp // 4, lax.rem(z, 4), group)

    def gain_copies(level, arriving):
        copies = []
        for step in range(1, 4):
            if level == 0:
                target = {"dp": row_peer(dp, step)}
            elif level == 1:
                target = {"dp": column_peer(dp, step)}
            elif level == 2:
                target = {"seq": chip(group * 4 + lax.rem(z + step, 4))}
            else:
                target = {"seq": chip(lax.rem(z + 4 * step, CHIPS))}
            there = lax.rem(places[level] + step, 4)
            slot = there if arriving else places[level]
            copies.append(
                pltpu.make_async_remote_copy(
                    gain_out.at[level], gain_in.at[level, slot], g_send.at[level, there], g_recv.at[level, slot],
                    device_id=target, device_id_type=MESH,
                )
            )
        return copies

    def send_gain(level, value):
        gain_out[level] = value
        gain_in[level, places[level]] = value
        for copy in gain_copies(level, False):
            copy.start()

    def gain_arrived(level):
        for copy in gain_copies(level, True):
            copy.wait_recv()
        return jnp.sum(gain_in[level], axis=0)

    gain_swap.wait_recv()
    send_gain(0, gain_own[...] + gain_oth[...])

    head_i = lax.broadcasted_iota(jnp.int32, (LANES, HEADS), 1)
    half_i = (lax.broadcasted_iota(jnp.int32, (LANES, HEADS), 0) >= HALF).astype(jnp.int32)
    column_i = lax.broadcasted_iota(jnp.int32, (TOK, HEADS), 1)

    def head_of(pair):
        return (head_i == 2 * pair + half_i).astype(BF16)

    later = jnp.zeros((TOK, HEADS), F32)
    for pair in range(PAIRS):
        if pair == MINE:
            send_gain(1, gain_arrived(0))
        q, k, v = q_s[:, lanes(pair)], k_s[:, lanes(pair)], v_s[:, lanes(pair)]
        mixed = g_s[pair]
        pairs = mm_t(stack(mixed), v)
        grad_weights = (pairs * p_s[pair]).astype(BF16)
        k_2 = stack(k)
        query_state = block_diagonal(si_s[pair]).astype(BF16)
        dq = mm(grad_weights[:TOK], k_2[:TOK]) + mm(grad_weights[TOK:], k_2[TOK:]) + entry_s[pair] * mm_t(mixed, query_state)
        dq_ref[:, lanes(pair)] = dq.astype(BF16)
        pairs_t = mm_t(stack(v), mixed)
        grad_weights_t = (pairs_t * pt_s[pair]).astype(BF16)
        q_2 = stack(q)
        dkl_s[pair] = mm(grad_weights_t[:TOK], q_2[:TOK]) + mm(grad_weights_t[TOK:], q_2[TOK:])
        weights_t = spt_s[pair].astype(BF16)
        g_2 = stack(mixed)
        dvl_s[pair] = mm(weights_t[:TOK], g_2[:TOK]) + mm(weights_t[TOK:], g_2[TOK:])
        balance = jnp.sum(sp_s[pair] * pairs - spt_s[pair] * pairs_t, axis=1, keepdims=True)
        later = later + jnp.where(column_i == 2 * pair, balance[:TOK], 0.0)
        later = later + jnp.where(column_i == 2 * pair + 1, balance[TOK:], 0.0)
        later = later + split_mm(car_s[pair] * mixed.astype(F32), head_of(pair))

    send_gain(2, gain_arrived(1))

    state = jnp.zeros((ROWS, LANES), F32)
    for there in reversed(range(1, CHIPS)):

        @pl.when(z != there)
        def _():
            from_chip(2, send3.at[there], recv3, there).wait_recv()

        state = recv3[there] if there == CHIPS - 1 else recv1[there, ROWS : ROWS + 1, :] * state + recv3[there]
        send4[there - 1] = state
    for there in (1, 0, 2, 3, 4, 5, 6, 7, 14, 13, 12, 11, 10, 9, 8):

        @pl.when(z != there)
        def _():
            to_chip(3, send4.at[there], recv4, there).start()

    @pl.when(z != CHIPS - 1)
    def _():
        recv4[z] = send4[z]

    @pl.when(z == CHIPS - 1)
    def _():
        recv4[...] = jnp.zeros_like(recv4)

    send_gain(3, gain_arrived(2))

    later_sum = split_mm_left((row_i <= col_i).astype(BF16), later)

    grad_swaps = []
    for i, pair in enumerate(near_pairs):
        wait_slices(3, pair, send4, recv4)
        index = MINE * core + pair
        _, s_1 = in_order(qs_own[index], qs_oth[pair])
        _, c_1 = carries(pair)
        arrived = recv4[pl.ds(pair * 4, 4)].reshape(HALF, LANES)
        own, other = in_order(s_1 + c_1 * arrived, arrived)
        sg_s[index] = own
        sg_x[pair] = other
        grad_swaps.append(to_partner(sg_x.at[pair], sg_s.at[index], 14 + i))
        grad_swaps[-1].start()

    earlier = jnp.zeros((TOK + 8, HEADS), F32)

    def finish(pair, earlier):
        k, v = k_s[:, lanes(pair)], v_s[:, lanes(pair)]
        state_grad = block_diagonal(sg_s[pair])
        dk_ref[:, lanes(pair)] = (dkl_s[pair] + exit_s[pair] * mm_t(v, state_grad.astype(BF16))).astype(BF16)
        carried_value = exit_s[pair] * split_mm_left(k, state_grad)
        dv_ref[:, lanes(pair)] = (dvl_s[pair] + carried_value).astype(BF16)
        through = jnp.sum(si_s[pair] * sg_s[pair], axis=0, keepdims=True) * carr_own[pl.ds(pair, 1), :]
        terms = jnp.concatenate([carried_value * v.astype(F32), jnp.broadcast_to(through, (8, LANES))], axis=0)
        return earlier + split_mm(terms, head_of(pair))

    for pair in range(MINE):
        earlier = finish(MINE * core + pair, earlier)
    for swap in grad_swaps:
        swap.wait_recv()
    for pair in range(MINE):
        earlier = finish(MINE * (1 - core) + pair, earlier)
    total = later_sum + split_mm_left((row_i > col_i).astype(BF16), earlier[:TOK]) + earlier[TOK : TOK + 1]
    dd_ref[...] = total.T
    dg_ref[...] = gain_arrived(3)

    for swap in (carry_swap, gain_swap, *state_swaps, *in_swaps, *query_swaps, *grad_swaps):
        swap.wait_send()
    for step in range(1, CHIPS):
        there = lax.rem(z + step, CHIPS)
        copies = (
            to_chip(0, send1.at[there, pl.ds(0, SENT)], recv1.at[:, pl.ds(0, SENT)], there),
            to_chip(1, send2.at[there], recv2, there),
            to_chip(2, send3.at[there], recv3, there),
            to_chip(3, send4.at[there], recv4, there),
        )
        for phase, copy in enumerate(copies):

            @pl.when((there if phase % 2 else z) != unsent[phase])
            def _(copy=copy):
                copy.wait_send()

    for level in range(4):
        for copy in gain_copies(level, False):
            copy.wait_send()


def write_out(*refs):
    sources, targets, sem = refs[:6], refs[6:12], refs[12]
    copies = [pltpu.make_async_copy(source, target, sem.at[i]) for i, (source, target) in enumerate(zip(sources, targets))]
    for copy in copies:
        copy.start()
    for copy in copies:
        copy.wait()


def local(queries, key_vectors, value_vectors, log_decay, restart, norm_gain, upstream):
    width = queries.shape[-1]
    vmem = pl.BlockSpec(memory_space=pltpu.VMEM)
    hbm = pl.BlockSpec(memory_space=pltpu.HBM)
    wide = pltpu.VMEM((TOK, width), BF16)
    table = pltpu.VMEM((PAIRS, TOK, LANES), F32)
    table_bf16 = pltpu.VMEM((PAIRS, TOK, LANES), BF16)
    double = pltpu.VMEM((PAIRS, 2 * TOK, LANES), F32)
    states = pltpu.VMEM((PAIRS, HALF, LANES), F32)
    some_states = pltpu.VMEM((MINE, HALF, LANES), F32)
    tile = pltpu.VMEM((8, LANES), F32)
    slices = pltpu.VMEM((CHIPS, ROWS, LANES), F32)
    slices_and = pltpu.VMEM((CHIPS, ROWS + 8, LANES), F32)
    dma = pltpu.SemaphoreType.DMA
    rows = jax.ShapeDtypeStruct((TOK, width), BF16)
    results = (
        rows, rows, rows, rows,
        jax.ShapeDtypeStruct((HEADS, TOK), F32),
        jax.ShapeDtypeStruct((8, LANES), F32),
    )
    outs = pl.pallas_call(
        kernel,
        out_shape=results,
        in_specs=[hbm] * 7,
        out_specs=[vmem] * 6,
        scratch_shapes=[
            wide, wide, wide, wide,
            pltpu.VMEM((HEADS, TOK), F32), pltpu.VMEM((1, TOK), jnp.int32), tile, dma((7,)),
            table, table, double, double, double, double, table, table, table_bf16, table_bf16, table_bf16, table, table,
            states, some_states, states, some_states, tile, tile, states, some_states, states, some_states,
            slices_and, slices_and, slices, slices, slices, slices, slices, slices,
            tile, tile, pltpu.VMEM((4, 8, LANES), F32), pltpu.VMEM((4, 4, 8, LANES), F32),
            dma((18,)), dma((18,)), dma((4, CHIPS)), dma((4, CHIPS)), dma((4, 4)), dma((4, 4)),
        ],
        compiler_params=pltpu.CompilerParams(collective_id=0, has_side_effects=True, vmem_limit_bytes=32 * 1024 * 1024),
    )(
        *(
            pltpu.with_memory_space_constraint(array, pltpu.HBM)
            for array in (
                queries[0], key_vectors[0], value_vectors[0], upstream[0],
                log_decay[0].T, restart, norm_gain.reshape(8, LANES),
            )
        )
    )
    layer_out, dq, dk, dv, dd, dg = pl.pallas_call(
        write_out,
        out_shape=tuple(pltpu.HBM(result.shape, result.dtype) for result in results),
        in_specs=[vmem] * 6,
        out_specs=[hbm] * 6,
        scratch_shapes=[dma((6,))],
    )(*(pltpu.with_memory_space_constraint(array, pltpu.VMEM) for array in outs))
    return (layer_out[None], dq[None], dk[None], dv[None], dd.T[None], dg.reshape(-1))


def solution(mesh):
    row, narrow = P("dp", "seq", None), P("dp", "seq")
    return jax.shard_map(
        local,
        mesh=mesh,
        in_specs=(row, row, row, row, narrow, P(), row),
        out_specs=(row, row, row, row, row, P()),
        check_vma=False,
    )
```
